32 devices in a mesh: gx: 2 (over y), gy: 4 (over z), gz: 4 (over x, core).
Axes of the slice: x: 2, y: 2, z: 4, core: 2. Of those that a mesh axis runs over, the one named last changes fastest.
Arguments:
- vel_u: bfloat16 [96, 8, 16, 512], P(None, 'gx', 'gy', 'gz'), may hold values from -300 to 300
- vel_v: bfloat16 [96, 8, 16, 512], P(None, 'gx', 'gy', 'gz'), may hold values from -300 to 300
- vel_w: bfloat16 [96, 8, 16, 512], P(None, 'gx', 'gy', 'gz'), may hold values from -300 to 300
- density: bfloat16 [96, 8, 16, 512], P(None, 'gx', 'gy', 'gz'), may hold values from -300 to 300
Outputs:
- basis: float32 [96, 2, 8, 16, 512], P(None, None, 'gx', 'gy', 'gz')
- factor: float32 [96, 96], replicated
The draws below stay inside these ranges and needn't reach their ends.
All inputs are finite; a program needn't handle non-finite values.
Results may differ from the reference program's by a relative error of at most 0.0015.
Values may be sent and summed in bfloat16 or wider, within the bound.
No kernel may reach another device: no remote copies, remote signals or barrier semaphores. Data moves between devices by JAX's collectives and lax.ppermute only.
A program may use at most 128 MiB of HBM per device.

```python
import math
import jax
import jax.numpy as jnp
from jax import lax

SNAPS = 96
NX = 8
NY = 16
NZ = 512


def snapshot_field(key, salt):
    folded = jax.random.fold_in(key, salt)
    key_rows, key_cols, key_vals = jax.random.split(folded, 3)
    plane_scale = jnp.exp(math.log(10.0) * jax.random.uniform(key_rows, (NX,), jnp.float32))
    snap_scale = jnp.exp(math.log(10.0) * jax.random.uniform(key_cols, (SNAPS,), jnp.float32))
    shape_all = (SNAPS, NX, NY, NZ)
    values_base = jnp.clip(jax.random.normal(key_vals, shape_all, jnp.float32), -3.0, 3.0)
    scaled = values_base * snap_scale[:, None, None, None] * plane_scale[None, :, None, None]
    return scaled.astype(jnp.bfloat16)


def draw_vel_u(key, part):
    return snapshot_field(key, 11)


def draw_vel_v(key, part):
    return snapshot_field(key, 23)


def draw_vel_w(key, part):
    return snapshot_field(key, 37)


def draw_density(key, part):
    return snapshot_field(key, 41)


def setup_inputs(seed: int = 0) -> dict:
    streams_of = jax.random.split(jax.random.key(seed), 5)
    vel_u = draw_vel_u(jax.random.fold_in(streams_of[4], 71), 0)
    vel_v = draw_vel_v(jax.random.fold_in(streams_of[4], 71), 0)
    vel_w = draw_vel_w(jax.random.fold_in(streams_of[4], 71), 0)
    density = draw_density(jax.random.fold_in(streams_of[4], 71), 0)
    return {"vel_u": vel_u, "vel_v": vel_v, "vel_w": vel_w, "density": density}


def ghost_cells(values):
    values = values.astype(jnp.float32)
    edged = jnp.pad(values, ((1, 1), (1, 1), (0, 0)), mode='edge')
    return jnp.pad(edged, ((0, 0), (0, 0), (1, 1)), mode='wrap')

def derive(snapshot):
    pad_u = ghost_cells(snapshot[0])
    pad_v = ghost_cells(snapshot[1])
    pad_w = ghost_cells(snapshot[2])
    pad_rho = ghost_cells(snapshot[3])
    diff_u = pad_u[2:, 1:-1, 1:-1] - pad_u[:-2, 1:-1, 1:-1]
    diff_v = pad_v[1:-1, 2:, 1:-1] - pad_v[1:-1, :-2, 1:-1]
    diff_w = pad_w[1:-1, 1:-1, 2:] - pad_w[1:-1, 1:-1, :-2]
    rho_x = pad_rho[2:, 1:-1, 1:-1] - pad_rho[:-2, 1:-1, 1:-1]
    rho_y = pad_rho[1:-1, 2:, 1:-1] - pad_rho[1:-1, :-2, 1:-1]
    rho_z = pad_rho[1:-1, 1:-1, 2:] - pad_rho[1:-1, 1:-1, :-2]
    dilatation = 0.5 * (diff_u + diff_v + diff_w)
    gradient = jnp.sqrt(0.25 * (rho_x * rho_x + rho_y * rho_y + rho_z * rho_z) + 0.25)
    return jnp.stack([dilatation, gradient])

def reference(vel_u, vel_v, vel_w, density):
    derived = lax.map(derive, (vel_u, vel_v, vel_w, density))
    panel = derived.reshape(SNAPS, -1)
    count = 2 * NX * NY * NZ
    moments = jnp.dot(panel.astype(jnp.float32), panel.T.astype(jnp.float32), precision=lax.Precision.HIGHEST, preferred_element_type=jnp.float32) / count
    lower = jnp.linalg.cholesky(moments)
    basis = jax.scipy.linalg.solve_triangular(lower, panel, lower=True).reshape(derived.shape)
    return (basis, lower.T)
```

```python
import functools

import jax
import jax.numpy as jnp
from jax import lax
from jax.experimental import pallas as pl
from jax.experimental.pallas import tpu as pltpu
from jax.sharding import PartitionSpec as P

F32 = jnp.float32
BF16 = jnp.bfloat16
LANES = 128
VMEM = pl.BlockSpec(memory_space=pltpu.VMEM)


def pairs(count, first, periodic):
    out = []
    for low in range(first, count - 1, 2):
        out += [(low, low + 1), (low + 1, low)]
    if first and periodic:
        out += [(count - 1, 0), (0, count - 1)]
    return out


def lane_index(rows):
    return lax.broadcasted_iota(jnp.int32, (rows, LANES), 1)


def pack_kernel(dims, u, v, w, rho, fields, x0, x1, y0, y1, z0, z1, wide):
    snaps, nx, ny = dims
    cells = nx * ny
    x_even = lax.axis_index("gx") % 2 == 0
    y_even = lax.axis_index("gy") % 2 == 0
    z_even = lax.axis_index("gz") % 2 == 0
    lane = lane_index(snaps)
    column = jnp.zeros((snaps, LANES), F32)
    for f, ref in enumerate((u, v, w, rho)):
        wide[f] = ref[...].astype(F32)

    def row(f, r):
        return wide[f, pl.ds(r, snaps, stride=cells), :]

    for f in range(4):
        for r in range(cells):
            cell = row(f, r)
            fields[f, r] = cell.astype(BF16)
            if f >= 2:
                k = (f - 2) * cells + r
                moved = pltpu.roll(cell, 2 * k + 1, 1)
                column = jnp.where((lane == 2 * k) | (lane == 2 * k + 1), moved, column)
    for i, f in enumerate((0, 3)):
        for y in range(ny):
            first, final = fields[f, y], fields[f, (nx - 1) * ny + y]
            x0[i, y] = jnp.where(x_even, final, first)
            x1[i, y] = jnp.where(x_even, first, final)
    for i, f in enumerate((1, 3)):
        for x in range(nx):
            first, final = fields[f, x * ny], fields[f, x * ny + ny - 1]
            y0[i, x] = jnp.where(y_even, final, first)
            y1[i, x] = jnp.where(y_even, first, final)
    final = jnp.where(lane % 2 == 0, column, 0.0)
    first = jnp.where(lane % 2 == 1, column, 0.0)
    z0[...] = jnp.where(z_even, final, first).astype(BF16)
    z1[...] = jnp.where(z_even, first, final).astype(BF16)


def panel_kernel(dims, scale, sizes, fields, x0, x1, y0, y1, z0, z1, panel, moments):
    snaps, nx, ny = dims
    cells = nx * ny
    at_x, at_y = lax.axis_index("gx"), lax.axis_index("gy")
    x_even, y_even = at_x % 2 == 0, at_y % 2 == 0
    lane = lane_index(snaps)
    edges = z0[...].astype(F32) + z1[...].astype(F32)

    def cell(f, r):
        return fields[f, r].astype(F32)

    def side(even, edge, own, recv_even, recv_odd):
        return jnp.where(edge, own, jnp.where(even, recv_even, recv_odd)).astype(F32)

    def diff_x(f, i, x, y):
        r = x * ny + y
        if x == 0:
            left = side(x_even, at_x == 0, fields[f, y], x1[i, y], x0[i, y])
        else:
            left = cell(f, r - ny)
        if x == nx - 1:
            right = side(x_even, at_x == sizes[0] - 1, fields[f, r], x0[i, y], x1[i, y])
        else:
            right = cell(f, r + ny)
        return right - left

    def diff_y(f, i, x, y):
        r = x * ny + y
        if y == 0:
            left = side(y_even, at_y == 0, fields[f, r], y1[i, x], y0[i, x])
        else:
            left = cell(f, r - 1)
        if y == ny - 1:
            right = side(y_even, at_y == sizes[1] - 1, fields[f, r], y0[i, x], y1[i, x])
        else:
            right = cell(f, r + 1)
        return right - left

    def diff_z(f, i, r):
        k = i * cells + r
        value = cell(f, r)
        ends = jnp.take_along_axis(
            edges, jnp.where(lane == LANES - 1, 2 * k + 1, 2 * k), axis=1
        )
        left = jnp.where(lane == 0, ends, pltpu.roll(value, 1, 1))
        right = jnp.where(lane == LANES - 1, ends, pltpu.roll(value, LANES - 1, 1))
        return right - left

    def put(c, value):
        high = value.astype(BF16)
        panel[0:snaps, c * LANES : (c + 1) * LANES] = high
        panel[snaps : 2 * snaps, c * LANES : (c + 1) * LANES] = (
            value - high.astype(F32)
        ).astype(BF16)

    for x in range(nx):
        for y in range(ny):
            r = x * ny + y
            dilatation = 0.5 * (diff_x(0, 0, x, y) + diff_y(1, 0, x, y) + diff_z(2, 0, r))
            put(r, dilatation)
            rx, ry, rz = diff_x(3, 1, x, y), diff_y(3, 1, x, y), diff_z(3, 1, r)
            put(cells + r, jnp.sqrt(0.25 * (rx * rx + ry * ry + rz * rz) + 0.25))

    def product(a, b):
        return lax.dot_general(a, b, (((1,), (1,)), ((), ())), preferred_element_type=F32)

    high, low = panel[0:snaps, :], panel[snaps : 2 * snaps, :]
    moments[...] = (product(high, high) + product(high, low) + product(low, high)) * scale


def basis_kernel(dims, moments, panel, basis, factor, work, inverse):
    snaps, nx, ny = dims
    cells = 2 * nx * ny
    lane = lane_index(8)
    sub = lax.broadcasted_iota(jnp.int32, (8, LANES), 0)
    groups = snaps // 8
    work[...] = jnp.zeros_like(work)
    work[:, 0:snaps] = moments[...]

    def spread(value, j):
        return jnp.broadcast_to(value[:, j : j + 1], (8, LANES))

    for g in range(groups):
        base = 8 * g
        rows = [jnp.broadcast_to(work[base + i : base + i + 1, :], (8, LANES)) for i in range(8)]
        small = [[spread(rows[i], base + j) for j in range(i + 1)] for i in range(8)]
        ratio = []
        for j in range(8):
            here = base + j
            root = lax.rsqrt(small[j][j])
            inv = root * root
            ratio.append(inv)
            pivot = jnp.where(lane == here, 1.0, rows[j])
            for i in range(j + 1, 8):
                m = small[i][j] * inv
                rows[i] = jnp.where(lane == here, 0.0, rows[i]) - m * pivot
                for k in range(j + 1, i + 1):
                    small[i][k] = small[i][k] - m * small[k][j]
            scaled = rows[j] * root
            factor[here : here + 1, :] = jnp.where(lane >= here, scaled, 0.0)[0:1, 0:snaps]
            inverse[here : here + 1, :] = jnp.where(
                lane < here, scaled, jnp.where(lane == here, root, 0.0)
            )[0:1, :]
        outer = []
        for j in range(8):
            here = base + j
            clean = jnp.where((lane > here) & (lane < base + 8), 0.0, rows[j])
            outer.append(jnp.where(lane == here, 1.0, clean))
        inside = (lane >= base) & (lane < base + 8)
        for h in range(g + 1, groups):
            block = jnp.where(inside, 0.0, work[8 * h : 8 * h + 8, :])
            for j in range(8):
                m = jnp.take_along_axis(rows[j] * ratio[j], sub + 8 * h, axis=1)
                block = block - m * outer[j]
            work[8 * h : 8 * h + 8, :] = block

    low_inv = inverse[:, 0:snaps]
    high = low_inv.astype(BF16)
    rest = (low_inv - high.astype(F32)).astype(BF16)
    left = jnp.concatenate([high, high], axis=1)
    for c in range(cells):
        block = panel[:, c * LANES : (c + 1) * LANES]
        out = jnp.dot(left, block, preferred_element_type=F32) + jnp.dot(
            rest, block[0:snaps, :], preferred_element_type=F32
        )
        basis[pl.ds(c, snaps, stride=cells), :] = out


def swap(value, axis, first, periodic=False):
    return lax.ppermute(value, axis, pairs(lax.axis_size(axis), first, periodic))


def total_over(value, axis):
    count = lax.axis_size(axis)
    if count & (count - 1):
        return lax.psum(value, axis)
    step = 1
    while step < count:
        value = value + lax.ppermute(value, axis, [(i, i ^ step) for i in range(count)])
        step *= 2
    return value


def per_device(vel_u, vel_v, vel_w, density):
    snaps, nx, ny, nz = vel_u.shape
    cells = nx * ny
    dims = (snaps, nx, ny)
    sizes = tuple(lax.axis_size(a) for a in ("gx", "gy", "gz"))
    flat = [a.reshape(snaps * cells, nz) for a in (vel_u, vel_v, vel_w, density)]
    params = pltpu.CompilerParams(vmem_limit_bytes=48 << 20)
    x_face = jax.ShapeDtypeStruct((2, ny, snaps, nz), BF16)
    y_face = jax.ShapeDtypeStruct((2, nx, snaps, nz), BF16)
    z_face = jax.ShapeDtypeStruct((snaps, nz), BF16)
    fields, x0, x1, y0, y1, z0, z1 = pl.pallas_call(
        functools.partial(pack_kernel, dims),
        out_shape=(
            jax.ShapeDtypeStruct((4, cells, snaps, nz), BF16),
            x_face,
            x_face,
            y_face,
            y_face,
            z_face,
            z_face,
        ),
        in_specs=[VMEM] * 4,
        out_specs=[VMEM] * 7,
        scratch_shapes=[pltpu.VMEM((4, snaps * cells, nz), F32)],
        compiler_params=params,
        name="pack",
    )(*flat)
    x0 = swap(x0, "gx", 0)
    y0 = swap(y0, "gy", 0)
    if sizes[1] > 2:
        y1 = swap(y1, "gy", 1)
    z0 = swap(z0, "gz", 0)
    z1 = swap(z1, "gz", 1, True)
    if sizes[0] > 2:
        x1 = swap(x1, "gx", 1)
    scale = 1.0 / (2 * cells * nz * sizes[0] * sizes[1] * sizes[2])
    panel, moments = pl.pallas_call(
        functools.partial(panel_kernel, dims, scale, sizes),
        out_shape=(
            jax.ShapeDtypeStruct((2 * snaps, 2 * cells * nz), BF16),
            jax.ShapeDtypeStruct((snaps, snaps), F32),
        ),
        in_specs=[VMEM] * 7,
        out_specs=[VMEM] * 2,
        compiler_params=params,
        name="panel",
    )(fields, x0, x1, y0, y1, z0, z1)
    for axis in ("gz", "gy", "gx"):
        moments = total_over(moments, axis)
    basis, factor = pl.pallas_call(
        functools.partial(basis_kernel, dims),
        out_shape=(
            jax.ShapeDtypeStruct((snaps * 2 * cells, nz), F32),
            jax.ShapeDtypeStruct((snaps, snaps), F32),
        ),
        in_specs=[VMEM] * 2,
        out_specs=[VMEM] * 2,
        scratch_shapes=[pltpu.VMEM((snaps, LANES), F32), pltpu.VMEM((snaps, LANES), F32)],
        compiler_params=params,
        name="basis",
    )(moments, panel)
    return basis.reshape(snaps, 2, nx, ny, nz), factor


def solution(mesh):
    spec = P(None, "gx", "gy", "gz")
    return jax.shard_map(
        per_device,
        mesh=mesh,
        in_specs=(spec,) * 4,
        out_specs=(P(None, None, "gx", "gy", "gz"), P()),
        check_vma=False,
    )
```

```python
import functools

import jax
import jax.numpy as jnp
from jax import lax
from jax.experimental import pallas as pl
from jax.experimental.pallas import tpu as pltpu
from jax.sharding import PartitionSpec as P

F32 = jnp.float32
BF16 = jnp.bfloat16
LANES = 128
VMEM = pl.BlockSpec(memory_space=pltpu.VMEM)
HBM = pl.BlockSpec(memory_space=pltpu.HBM)


def pairs(count, first, periodic):
    out = []
    for low in range(first, count - 1, 2):
        out += [(low, low + 1), (low + 1, low)]
    if first and periodic:
        out += [(count - 1, 0), (0, count - 1)]
    return out


def lane_index(rows):
    return lax.broadcasted_iota(jnp.int32, (rows, LANES), 1)


def fold(full):
    full = jnp.concatenate([full, jnp.zeros((96, LANES - 96), F32)], axis=1)
    top, rest = full[0:48], full[48:96]
    lane = lane_index(48)
    near = pltpu.roll(rest, 48, 1)
    far = pltpu.roll(rest, 64, 1)
    top = jnp.where(lane >= 96, near, top)
    lane = lane_index(16)
    middle = jnp.where(lane < 16, near[32:48], top[16:32])
    bottom = jnp.where(lane < 16, near[0:16], jnp.where(lane < 32, far[16:32], top[32:48]))
    return jnp.concatenate([top[0:16], middle, bottom], axis=0)


def unfold(folded, work):
    lane = lane_index(16)
    near = pltpu.roll(folded, 80, 1)
    far = pltpu.roll(folded[32:48], 64, 1)
    work[0:48, :] = folded
    work[48:64, :] = jnp.where(lane < 80, near[0:16], near[32:48])
    work[64:80, :] = jnp.where(lane < 80, near[16:32], far)
    work[80:96, :] = jnp.where(lane < 80, near[32:48], near[16:32])


def pack_kernel(dims, u, v, w, rho, fields, x0, x1, y0, y1, z0, z1, narrow, wide, arrived):
    snaps, nx, ny = dims
    cells = nx * ny
    copies = [
        pltpu.make_async_copy(ref, narrow.at[f], arrived.at[f])
        for f, ref in enumerate((u, v, w, rho))
    ]
    for copy in copies:
        copy.start()
    x_even = lax.axis_index("gx") % 2 == 0
    y_even = lax.axis_index("gy") % 2 == 0
    z_even = lax.axis_index("gz") % 2 == 0
    lane = lane_index(snaps)
    column = jnp.zeros((snaps, LANES), F32)

    def row(f, r):
        return wide[f, pl.ds(r, snaps, stride=cells), :]

    for f in range(4):
        copies[f].wait()
        wide[f] = narrow[f].astype(F32)
        for r in range(cells):
            cell = row(f, r)
            fields[f, r] = cell.astype(BF16)
            if f >= 2:
                k = (f - 2) * cells + r
                moved = pltpu.roll(cell, 2 * k + 1, 1)
                column = jnp.where((lane == 2 * k) | (lane == 2 * k + 1), moved, column)
    for i, f in enumerate((0, 3)):
        for y in range(ny):
            first, final = fields[f, y], fields[f, (nx - 1) * ny + y]
            x0[i, y] = jnp.where(x_even, final, first)
            x1[i, y] = jnp.where(x_even, first, final)
    for i, f in enumerate((1, 3)):
        for x in range(nx):
            first, final = fields[f, x * ny], fields[f, x * ny + ny - 1]
            y0[i, x] = jnp.where(y_even, final, first)
            y1[i, x] = jnp.where(y_even, first, final)
    final = jnp.where(lane % 2 == 0, column, 0.0)
    first = jnp.where(lane % 2 == 1, column, 0.0)
    z0[...] = jnp.where(z_even, final, first).astype(BF16)
    z1[...] = jnp.where(z_even, first, final).astype(BF16)


def panel_kernel(dims, scale, sizes, fields, x0, x1, y0, y1, z0, z1, panel, moments):
    snaps, nx, ny = dims
    cells = nx * ny
    at_x, at_y = lax.axis_index("gx"), lax.axis_index("gy")
    x_even, y_even = at_x % 2 == 0, at_y % 2 == 0
    lane = lane_index(snaps)
    edges = z0[...].astype(F32) + z1[...].astype(F32)

    def cell(f, r):
        return fields[f, r].astype(F32)

    def side(even, edge, own, recv_even, recv_odd):
        return jnp.where(edge, own, jnp.where(even, recv_even, recv_odd)).astype(F32)

    def diff_x(f, i, x, y):
        r = x * ny + y
        if x == 0:
            left = side(x_even, at_x == 0, fields[f, y], x1[i, y], x0[i, y])
        else:
            left = cell(f, r - ny)
        if x == nx - 1:
            right = side(x_even, at_x == sizes[0] - 1, fields[f, r], x0[i, y], x1[i, y])
        else:
            right = cell(f, r + ny)
        return right - left

    def diff_y(f, i, x, y):
        r = x * ny + y
        if y == 0:
            left = side(y_even, at_y == 0, fields[f, r], y1[i, x], y0[i, x])
        else:
            left = cell(f, r - 1)
        if y == ny - 1:
            right = side(y_even, at_y == sizes[1] - 1, fields[f, r], y0[i, x], y1[i, x])
        else:
            right = cell(f, r + 1)
        return right - left

    def diff_z(f, i, r):
        k = i * cells + r
        value = cell(f, r)
        ends = jnp.take_along_axis(
            edges, jnp.where(lane == LANES - 1, 2 * k + 1, 2 * k), axis=1
        )
        left = jnp.where(lane == 0, ends, pltpu.roll(value, 1, 1))
        right = jnp.where(lane == LANES - 1, ends, pltpu.roll(value, LANES - 1, 1))
        return right - left

    def put(c, value):
        high = value.astype(BF16)
        panel[0:snaps, c * LANES : (c + 1) * LANES] = high
        panel[snaps : 2 * snaps, c * LANES : (c + 1) * LANES] = (
            value - high.astype(F32)
        ).astype(BF16)

    for x in range(nx):
        for y in range(ny):
            r = x * ny + y
            dilatation = 0.5 * (diff_x(0, 0, x, y) + diff_y(1, 0, x, y) + diff_z(2, 0, r))
            put(r, dilatation)
            rx, ry, rz = diff_x(3, 1, x, y), diff_y(3, 1, x, y), diff_z(3, 1, r)
            put(cells + r, jnp.sqrt(0.25 * (rx * rx + ry * ry + rz * rz) + 0.25))

    def product(a, b):
        return lax.dot_general(a, b, (((1,), (1,)), ((), ())), preferred_element_type=F32)

    high, low = panel[0:snaps, :], panel[snaps : 2 * snaps, :]
    total = (product(high, high) + product(high, low) + product(low, high)) * scale
    moments[...] = fold(total)


def basis_kernel(dims, moments, panel, basis, factor, work, inverse, ready, sent):
    snaps, nx, ny = dims
    cells = 2 * nx * ny
    lane = lane_index(8)
    sub = lax.broadcasted_iota(jnp.int32, (8, LANES), 0)
    groups = snaps // 8
    unfold(moments[...], work)

    def spread(value, j):
        return jnp.broadcast_to(value[:, j : j + 1], (8, LANES))

    for g in range(groups):
        base = 8 * g
        rows = [jnp.broadcast_to(work[base + i : base + i + 1, :], (8, LANES)) for i in range(8)]
        small = [[spread(rows[j], base + i) for j in range(i + 1)] for i in range(8)]
        ratio = []
        for j in range(8):
            here = base + j
            root = lax.rsqrt(small[j][j])
            inv = root * root
            ratio.append(inv)
            pivot = jnp.where(lane == here, 1.0, rows[j])
            for i in range(j + 1, 8):
                m = small[i][j] * inv
                rows[i] = jnp.where(lane == here, 0.0, rows[i]) - m * pivot
                for k in range(j + 1, i + 1):
                    small[i][k] = small[i][k] - m * small[k][j]
            scaled = rows[j] * root
            factor[here : here + 1, :] = jnp.where(lane >= here, scaled, 0.0)[0:1, 0:snaps]
            inverse[here : here + 1, :] = jnp.where(
                lane < here, scaled, jnp.where(lane == here, root, 0.0)
            )[0:1, :]
        outer = []
        for j in range(8):
            here = base + j
            clean = jnp.where((lane > here) & (lane < base + 8), 0.0, rows[j])
            outer.append(jnp.where(lane == here, 1.0, clean))
        inside = (lane >= base) & (lane < base + 8)
        for h in range(g + 1, groups):
            block = jnp.where(inside, 0.0, work[8 * h : 8 * h + 8, :])
            for j in range(8):
                m = jnp.take_along_axis(rows[j] * ratio[j], sub + 8 * h, axis=1)
                block = block - m * outer[j]
            work[8 * h : 8 * h + 8, :] = block

    low_inv = inverse[:, 0:snaps]
    high = low_inv.astype(BF16)
    rest = (low_inv - high.astype(F32)).astype(BF16)
    left = jnp.concatenate(
        [
            jnp.concatenate([high, high], axis=1),
            jnp.concatenate([rest, jnp.zeros_like(rest)], axis=1),
        ],
        axis=0,
    )
    copies = []
    for k in range(cells // 8):
        for c in range(8 * k, 8 * k + 8, 2):
            both = jnp.dot(
                left, panel[:, c * LANES : (c + 2) * LANES], preferred_element_type=F32
            )
            out = both[0:snaps] + both[snaps : 2 * snaps]
            for i in range(2):
                ready[k, pl.ds(c % 8 + i, snaps, stride=8), :] = out[:, i * LANES : (i + 1) * LANES]
        copies.append(
            pltpu.make_async_copy(
                ready.at[k].reshape(snaps, 8, LANES), basis.at[:, 8 * k : 8 * k + 8, :], sent.at[k]
            )
        )
        copies[-1].start()
    for copy in copies:
        copy.wait()


def swap(value, axis, first, periodic=False):
    return lax.ppermute(value, axis, pairs(lax.axis_size(axis), first, periodic))


def total_over(value, axis):
    count = lax.axis_size(axis)
    if count & (count - 1):
        return lax.psum(value, axis)
    step = 1
    while step < count:
        value = value + lax.ppermute(value, axis, [(i, i ^ step) for i in range(count)])
        step *= 2
    return value


def per_device(vel_u, vel_v, vel_w, density):
    snaps, nx, ny, nz = vel_u.shape
    cells = nx * ny
    dims = (snaps, nx, ny)
    sizes = tuple(lax.axis_size(a) for a in ("gx", "gy", "gz"))
    flat = [
        pltpu.with_memory_space_constraint(a.reshape(snaps * cells, nz), pltpu.HBM)
        for a in (vel_u, vel_v, vel_w, density)
    ]
    params = pltpu.CompilerParams(vmem_limit_bytes=48 << 20)
    x_face = jax.ShapeDtypeStruct((2, ny, snaps, nz), BF16)
    y_face = jax.ShapeDtypeStruct((2, nx, snaps, nz), BF16)
    z_face = jax.ShapeDtypeStruct((snaps, nz), BF16)
    fields, x0, x1, y0, y1, z0, z1 = pl.pallas_call(
        functools.partial(pack_kernel, dims),
        out_shape=(
            jax.ShapeDtypeStruct((4, cells, snaps, nz), BF16),
            x_face,
            x_face,
            y_face,
            y_face,
            z_face,
            z_face,
        ),
        in_specs=[HBM] * 4,
        out_specs=[VMEM] * 7,
        scratch_shapes=[
            pltpu.VMEM((4, snaps * cells, nz), BF16),
            pltpu.VMEM((4, snaps * cells, nz), F32),
            pltpu.SemaphoreType.DMA((4,)),
        ],
        compiler_params=params,
        name="pack",
    )(*flat)
    x0 = swap(x0, "gx", 0)
    y0 = swap(y0, "gy", 0)
    if sizes[1] > 2:
        y1 = swap(y1, "gy", 1)
    z0 = swap(z0, "gz", 0)
    z1 = swap(z1, "gz", 1, True)
    if sizes[0] > 2:
        x1 = swap(x1, "gx", 1)
    scale = 1.0 / (2 * cells * nz * sizes[0] * sizes[1] * sizes[2])
    panel, moments = pl.pallas_call(
        functools.partial(panel_kernel, dims, scale, sizes),
        out_shape=(
            jax.ShapeDtypeStruct((2 * snaps, 2 * cells * nz), BF16),
            jax.ShapeDtypeStruct((snaps // 2, LANES), F32),
        ),
        in_specs=[VMEM] * 7,
        out_specs=[VMEM] * 2,
        compiler_params=params,
        name="panel",
    )(fields, x0, x1, y0, y1, z0, z1)
    for axis in ("gz", "gy", "gx"):
        moments = total_over(moments, axis)
    basis, factor = pl.pallas_call(
        functools.partial(basis_kernel, dims),
        out_shape=(
            jax.ShapeDtypeStruct((snaps, 2 * cells, nz), F32),
            jax.ShapeDtypeStruct((snaps, snaps), F32),
        ),
        in_specs=[VMEM] * 2,
        out_specs=[HBM, VMEM],
        scratch_shapes=[
            pltpu.VMEM((snaps, LANES), F32),
            pltpu.VMEM((snaps, LANES), F32),
            pltpu.VMEM((cells // 4, snaps * 8, nz), F32),
            pltpu.SemaphoreType.DMA((cells // 4,)),
        ],
        compiler_params=params,
        name="basis",
    )(moments, panel)
    return basis.reshape(snaps, 2, nx, ny, nz), factor


def solution(mesh):
    spec = P(None, "gx", "gy", "gz")
    return jax.shard_map(
        per_device,
        mesh=mesh,
        in_specs=(spec,) * 4,
        out_specs=(P(None, None, "gx", "gy", "gz"), P()),
        check_vma=False,
    )
```

```python
import functools

import jax
import jax.numpy as jnp
import numpy as np
from jax import lax
from jax.experimental import pallas as pl
from jax.experimental.pallas import tpu as pltpu
from jax.sharding import PartitionSpec as P

F32 = jnp.float32
BF16 = jnp.bfloat16
LANES = 128
VMEM = pl.BlockSpec(memory_space=pltpu.VMEM)
HBM = pl.BlockSpec(memory_space=pltpu.HBM)


AXES = ("gx", "gy", "gz")


def swapped(value, axis, first, periodic=False):
    sizes = [lax.axis_size(a) for a in AXES]
    where = AXES.index(axis)
    count = sizes[where]
    out = []
    for here in np.ndindex(*sizes):
        to = list(here)
        to[where] += 1 if here[where] % 2 == first else -1
        if periodic:
            to[where] %= count
        if not 0 <= to[where] < count:
            to = [here[0], here[1], here[2] ^ 1]
        out.append((int(np.ravel_multi_index(here, sizes)), int(np.ravel_multi_index(to, sizes))))
    return lax.ppermute(value, AXES, out)


def summed(value, mate):
    count = int(np.prod([lax.axis_size(a) for a in AXES]))
    if count & (count - 1):
        return lax.psum(value, AXES)
    steps = [mate] + [
        1 << k | mate for k in range(count.bit_length() - 1) if 1 << k != mate
    ]
    for step in steps:
        value = value + lax.ppermute(value, AXES, [(i, i ^ step) for i in range(count)])
    return value


def lane_index(rows):
    return lax.broadcasted_iota(jnp.int32, (rows, LANES), 1)


def fold(full):
    full = jnp.concatenate([full, jnp.zeros((96, LANES - 96), F32)], axis=1)
    top, rest = full[0:48], full[48:96]
    lane = lane_index(48)
    near = pltpu.roll(rest, 48, 1)
    far = pltpu.roll(rest, 64, 1)
    top = jnp.where(lane >= 96, near, top)
    lane = lane_index(16)
    middle = jnp.where(lane < 16, near[32:48], top[16:32])
    bottom = jnp.where(lane < 16, near[0:16], jnp.where(lane < 32, far[16:32], top[32:48]))
    return jnp.concatenate([top[0:16], middle, bottom], axis=0)


def unfold(folded, work):
    lane = lane_index(16)
    near = pltpu.roll(folded, 80, 1)
    far = pltpu.roll(folded[32:48], 64, 1)
    work[0:48, :] = folded
    work[48:64, :] = jnp.where(lane < 80, near[0:16], near[32:48])
    work[64:80, :] = jnp.where(lane < 80, near[16:32], far)
    work[80:96, :] = jnp.where(lane < 80, near[32:48], near[16:32])


def pack_kernel(dims, u, v, w, rho, fields, x0, x1, y0, y1, z0, z1, narrow, wide, arrived):
    snaps, nx, ny = dims
    cells = nx * ny
    copies = [
        pltpu.make_async_copy(ref, narrow.at[f], arrived.at[f])
        for f, ref in enumerate((u, v, w, rho))
    ]
    for copy in copies:
        copy.start()
    x_even = lax.axis_index("gx") % 2 == 0
    y_even = lax.axis_index("gy") % 2 == 0
    z_even = lax.axis_index("gz") % 2 == 0
    lane = lane_index(snaps)
    column = jnp.zeros((snaps, LANES), F32)

    def row(f, r):
        return wide[f, pl.ds(r, snaps, stride=cells), :]

    for f in range(4):
        copies[f].wait()
        wide[f] = narrow[f].astype(F32)
        for r in range(cells):
            cell = row(f, r)
            fields[f, r] = cell.astype(BF16)
            if f >= 2:
                k = (f - 2) * cells + r
                moved = pltpu.roll(cell, 2 * k + 1, 1)
                column = jnp.where((lane == 2 * k) | (lane == 2 * k + 1), moved, column)
    for i, f in enumerate((0, 3)):
        for y in range(ny):
            first, final = fields[f, y], fields[f, (nx - 1) * ny + y]
            x0[i, y] = jnp.where(x_even, final, first)
            x1[i, y] = jnp.where(x_even, first, final)
    for i, f in enumerate((1, 3)):
        for x in range(nx):
            first, final = fields[f, x * ny], fields[f, x * ny + ny - 1]
            y0[i, x] = jnp.where(y_even, final, first)
            y1[i, x] = jnp.where(y_even, first, final)
    final = jnp.where(lane % 2 == 0, column, 0.0)
    first = jnp.where(lane % 2 == 1, column, 0.0)
    z0[...] = jnp.where(z_even, final, first).astype(BF16)
    z1[...] = jnp.where(z_even, first, final).astype(BF16)


def panel_kernel(dims, scale, sizes, fields, x0, x1, y0, y1, z0, z1, panel, moments):
    snaps, nx, ny = dims
    cells = nx * ny
    at_x, at_y = lax.axis_index("gx"), lax.axis_index("gy")
    x_even, y_even = at_x % 2 == 0, at_y % 2 == 0
    lane = lane_index(snaps)
    edges = z0[...].astype(F32) + z1[...].astype(F32)

    def cell(f, r):
        return fields[f, r].astype(F32)

    def side(even, edge, own, recv_even, recv_odd):
        return jnp.where(edge, own, jnp.where(even, recv_even, recv_odd)).astype(F32)

    def diff_x(f, i, x, y):
        r = x * ny + y
        if x == 0:
            left = side(x_even, at_x == 0, fields[f, y], x1[i, y], x0[i, y])
        else:
            left = cell(f, r - ny)
        if x == nx - 1:
            right = side(x_even, at_x == sizes[0] - 1, fields[f, r], x0[i, y], x1[i, y])
        else:
            right = cell(f, r + ny)
        return right - left

    def diff_y(f, i, x, y):
        r = x * ny + y
        if y == 0:
            left = side(y_even, at_y == 0, fields[f, r], y1[i, x], y0[i, x])
        else:
            left = cell(f, r - 1)
        if y == ny - 1:
            right = side(y_even, at_y == sizes[1] - 1, fields[f, r], y0[i, x], y1[i, x])
        else:
            right = cell(f, r + 1)
        return right - left

    def diff_z(f, i, r):
        k = i * cells + r
        value = cell(f, r)
        ends = jnp.take_along_axis(
            edges, jnp.where(lane == LANES - 1, 2 * k + 1, 2 * k), axis=1
        )
        left = jnp.where(lane == 0, ends, pltpu.roll(value, 1, 1))
        right = jnp.where(lane == LANES - 1, ends, pltpu.roll(value, LANES - 1, 1))
        return right - left

    def put(c, value):
        high = value.astype(BF16)
        panel[0:snaps, c * LANES : (c + 1) * LANES] = high
        panel[snaps : 2 * snaps, c * LANES : (c + 1) * LANES] = (
            value - high.astype(F32)
        ).astype(BF16)

    for x in range(nx):
        for y in range(ny):
            r = x * ny + y
            dilatation = 0.5 * (diff_x(0, 0, x, y) + diff_y(1, 0, x, y) + diff_z(2, 0, r))
            put(r, dilatation)
            rx, ry, rz = diff_x(3, 1, x, y), diff_y(3, 1, x, y), diff_z(3, 1, r)
            put(cells + r, jnp.sqrt(0.25 * (rx * rx + ry * ry + rz * rz) + 0.25))

    def product(a, b):
        return lax.dot_general(a, b, (((1,), (1,)), ((), ())), preferred_element_type=F32)

    high, low = panel[0:snaps, :], panel[snaps : 2 * snaps, :]
    total = (product(high, high) + product(high, low) + product(low, high)) * scale
    moments[...] = fold(total)


def basis_kernel(dims, moments, panel, basis, factor, work, inverse, ready, sent):
    snaps, nx, ny = dims
    cells = 2 * nx * ny
    lane = lane_index(8)
    sub = lax.broadcasted_iota(jnp.int32, (8, LANES), 0)
    groups = snaps // 8
    unfold(moments[...], work)

    def spread(value, j):
        return jnp.broadcast_to(value[:, j : j + 1], (8, LANES))

    for g in range(groups):
        base = 8 * g
        rows = [jnp.broadcast_to(work[base + i : base + i + 1, :], (8, LANES)) for i in range(8)]
        small = [[spread(rows[j], base + i) for j in range(i + 1)] for i in range(8)]
        ratio = []
        for j in range(8):
            here = base + j
            root = lax.rsqrt(small[j][j])
            inv = root * root
            ratio.append(inv)
            pivot = jnp.where(lane == here, 1.0, rows[j])
            for i in range(j + 1, 8):
                m = small[i][j] * inv
                rows[i] = jnp.where(lane == here, 0.0, rows[i]) - m * pivot
                for k in range(j + 1, i + 1):
                    small[i][k] = small[i][k] - m * small[k][j]
            scaled = rows[j] * root
            factor[here : here + 1, :] = jnp.where(lane >= here, scaled, 0.0)[0:1, 0:snaps]
            inverse[here : here + 1, :] = jnp.where(
                lane < here, scaled, jnp.where(lane == here, root, 0.0)
            )[0:1, :]
        outer = []
        for j in range(8):
            here = base + j
            clean = jnp.where((lane > here) & (lane < base + 8), 0.0, rows[j])
            outer.append(jnp.where(lane == here, 1.0, clean))
        inside = (lane >= base) & (lane < base + 8)
        for h in range(g + 1, groups):
            block = jnp.where(inside, 0.0, work[8 * h : 8 * h + 8, :])
            for j in range(8):
                m = jnp.take_along_axis(rows[j] * ratio[j], sub + 8 * h, axis=1)
                block = block - m * outer[j]
            work[8 * h : 8 * h + 8, :] = block

    low_inv = inverse[:, 0:snaps]
    high = low_inv.astype(BF16)
    rest = (low_inv - high.astype(F32)).astype(BF16)
    left = jnp.concatenate(
        [
            jnp.concatenate([high, high], axis=1),
            jnp.concatenate([rest, jnp.zeros_like(rest)], axis=1),
        ],
        axis=0,
    )
    copies = []
    for k in range(cells // 8):
        for c in range(8 * k, 8 * k + 8, 2):
            both = jnp.dot(
                left, panel[:, c * LANES : (c + 2) * LANES], preferred_element_type=F32
            )
            out = both[0:snaps] + both[snaps : 2 * snaps]
            for i in range(2):
                ready[k, pl.ds(c % 8 + i, snaps, stride=8), :] = out[:, i * LANES : (i + 1) * LANES]
        copies.append(
            pltpu.make_async_copy(
                ready.at[k].reshape(snaps, 8, LANES), basis.at[:, 8 * k : 8 * k + 8, :], sent.at[k]
            )
        )
        copies[-1].start()
    for copy in copies:
        copy.wait()


def per_device(mate, vel_u, vel_v, vel_w, density):
    snaps, nx, ny, nz = vel_u.shape
    cells = nx * ny
    dims = (snaps, nx, ny)
    sizes = tuple(lax.axis_size(a) for a in AXES)
    flat = [
        pltpu.with_memory_space_constraint(a.reshape(snaps * cells, nz), pltpu.HBM)
        for a in (vel_u, vel_v, vel_w, density)
    ]
    params = pltpu.CompilerParams(vmem_limit_bytes=48 << 20)
    x_face = jax.ShapeDtypeStruct((2, ny, snaps, nz), BF16)
    y_face = jax.ShapeDtypeStruct((2, nx, snaps, nz), BF16)
    z_face = jax.ShapeDtypeStruct((snaps, nz), BF16)
    fields, x0, x1, y0, y1, z0, z1 = pl.pallas_call(
        functools.partial(pack_kernel, dims),
        out_shape=(
            jax.ShapeDtypeStruct((4, cells, snaps, nz), BF16),
            x_face,
            x_face,
            y_face,
            y_face,
            z_face,
            z_face,
        ),
        in_specs=[HBM] * 4,
        out_specs=[VMEM] * 7,
        scratch_shapes=[
            pltpu.VMEM((4, snaps * cells, nz), BF16),
            pltpu.VMEM((4, snaps * cells, nz), F32),
            pltpu.SemaphoreType.DMA((4,)),
        ],
        compiler_params=params,
        name="pack",
    )(*flat)
    x0 = swapped(x0, "gx", 0)
    y0 = swapped(y0, "gy", 0)
    if sizes[1] > 2:
        y1 = swapped(y1, "gy", 1)
    z0 = swapped(z0, "gz", 0)
    z1 = swapped(z1, "gz", 1, True)
    if sizes[0] > 2:
        x1 = swapped(x1, "gx", 1)
    scale = 1.0 / (2 * cells * nz * sizes[0] * sizes[1] * sizes[2])
    panel, moments = pl.pallas_call(
        functools.partial(panel_kernel, dims, scale, sizes),
        out_shape=(
            jax.ShapeDtypeStruct((2 * snaps, 2 * cells * nz), BF16),
            jax.ShapeDtypeStruct((snaps // 2, LANES), F32),
        ),
        in_specs=[VMEM] * 7,
        out_specs=[VMEM] * 2,
        compiler_params=params,
        name="panel",
    )(fields, x0, x1, y0, y1, z0, z1)
    moments = summed(moments, mate)
    basis, factor = pl.pallas_call(
        functools.partial(basis_kernel, dims),
        out_shape=(
            jax.ShapeDtypeStruct((snaps, 2 * cells, nz), F32),
            jax.ShapeDtypeStruct((snaps, snaps), F32),
        ),
        in_specs=[VMEM] * 2,
        out_specs=[HBM, VMEM],
        scratch_shapes=[
            pltpu.VMEM((snaps, LANES), F32),
            pltpu.VMEM((snaps, LANES), F32),
            pltpu.VMEM((cells // 4, snaps * 8, nz), F32),
            pltpu.SemaphoreType.DMA((cells // 4,)),
        ],
        compiler_params=params,
        name="basis",
    )(moments, panel)
    return basis.reshape(snaps, 2, nx, ny, nz), factor


def chip_mate(mesh):
    devices = list(mesh.devices.flat)
    at = [getattr(d, "coords", None) for d in devices]
    near = [k for k in range(1, len(at)) if at[0] is not None and at[k] == at[0]]
    return near[0] if near and near[0] & (near[0] - 1) == 0 else 1


def solution(mesh):
    spec = P(None, "gx", "gy", "gz")
    return jax.shard_map(
        functools.partial(per_device, chip_mate(mesh)),
        mesh=mesh,
        in_specs=(spec,) * 4,
        out_specs=(P(None, None, "gx", "gy", "gz"), P()),
        check_vma=False,
    )
```

```python
import functools

import jax
import jax.numpy as jnp
import numpy as np
from jax import lax
from jax.experimental import pallas as pl
from jax.experimental.pallas import tpu as pltpu
from jax.sharding import PartitionSpec as P

F32 = jnp.float32
BF16 = jnp.bfloat16
LANES = 128
CUTS = (0, 64)
VMEM = pl.BlockSpec(memory_space=pltpu.VMEM)
HBM = pl.BlockSpec(memory_space=pltpu.HBM)


AXES = ("gx", "gy", "gz")


def swapped(value, axis, first, periodic=False):
    sizes = [lax.axis_size(a) for a in AXES]
    where = AXES.index(axis)
    count = sizes[where]
    out = []
    for here in np.ndindex(*sizes):
        to = list(here)
        to[where] += 1 if here[where] % 2 == first else -1
        if periodic:
            to[where] %= count
        if not 0 <= to[where] < count:
            to = [here[0], here[1], here[2] ^ 1]
        out.append((int(np.ravel_multi_index(here, sizes)), int(np.ravel_multi_index(to, sizes))))
    return lax.ppermute(value, AXES, out)


def summed(value, mate):
    count = int(np.prod([lax.axis_size(a) for a in AXES]))
    if count & (count - 1):
        return lax.psum(value, AXES)
    steps = [mate] + [
        1 << k | mate for k in range(count.bit_length() - 1) if 1 << k != mate
    ]
    for step in steps:
        value = value + lax.ppermute(value, AXES, [(i, i ^ step) for i in range(count)])
    return value


def lane_index(rows):
    return lax.broadcasted_iota(jnp.int32, (rows, LANES), 1)


def fold(full):
    full = jnp.concatenate([full, jnp.zeros((96, LANES - 96), F32)], axis=1)
    top, rest = full[0:48], full[48:96]
    lane = lane_index(48)
    near = pltpu.roll(rest, 48, 1)
    far = pltpu.roll(rest, 64, 1)
    top = jnp.where(lane >= 96, near, top)
    lane = lane_index(16)
    middle = jnp.where(lane < 16, near[32:48], top[16:32])
    bottom = jnp.where(lane < 16, near[0:16], jnp.where(lane < 32, far[16:32], top[32:48]))
    return jnp.concatenate([top[0:16], middle, bottom], axis=0)


def unfold(folded, work):
    lane = lane_index(16)
    near = pltpu.roll(folded, 80, 1)
    far = pltpu.roll(folded[32:48], 64, 1)
    work[0:48, :] = folded
    work[48:64, :] = jnp.where(lane < 80, near[0:16], near[32:48])
    work[64:80, :] = jnp.where(lane < 80, near[16:32], far)
    work[80:96, :] = jnp.where(lane < 80, near[32:48], near[16:32])


def pack_kernel(dims, u, v, w, rho, fields, x0, x1, y0, y1, z0, z1, narrow, wide, arrived):
    snaps, nx, ny = dims
    cells = nx * ny
    copies = [
        pltpu.make_async_copy(ref, narrow.at[f], arrived.at[f])
        for f, ref in enumerate((u, v, w, rho))
    ]
    for copy in copies:
        copy.start()
    x_even = lax.axis_index("gx") % 2 == 0
    y_even = lax.axis_index("gy") % 2 == 0
    z_even = lax.axis_index("gz") % 2 == 0
    lane = lane_index(snaps)
    column = jnp.zeros((snaps, LANES), F32)

    def row(f, r):
        return wide[f, pl.ds(r, snaps, stride=cells), :]

    for f in range(4):
        copies[f].wait()
        wide[f] = narrow[f].astype(F32)
        for r in range(cells):
            cell = row(f, r)
            fields[f, r] = cell.astype(BF16)
            if f >= 2:
                k = (f - 2) * cells + r
                moved = pltpu.roll(cell, 2 * k + 1, 1)
                column = jnp.where((lane == 2 * k) | (lane == 2 * k + 1), moved, column)
    for i, f in enumerate((0, 3)):
        for y in range(ny):
            first, final = fields[f, y], fields[f, (nx - 1) * ny + y]
            x0[i, y] = jnp.where(x_even, final, first)
            x1[i, y] = jnp.where(x_even, first, final)
    for i, f in enumerate((1, 3)):
        for x in range(nx):
            first, final = fields[f, x * ny], fields[f, x * ny + ny - 1]
            y0[i, x] = jnp.where(y_even, final, first)
            y1[i, x] = jnp.where(y_even, first, final)
    final = jnp.where(lane % 2 == 0, column, 0.0)
    first = jnp.where(lane % 2 == 1, column, 0.0)
    z0[...] = jnp.where(z_even, final, first).astype(BF16)
    z1[...] = jnp.where(z_even, first, final).astype(BF16)


def panel_kernel(dims, scale, sizes, fields, x0, x1, y0, y1, z0, z1, panel, moments):
    snaps, nx, ny = dims
    cells = nx * ny
    at_x, at_y = lax.axis_index("gx"), lax.axis_index("gy")
    x_even, y_even = at_x % 2 == 0, at_y % 2 == 0
    lane = lane_index(snaps)
    edges = z0[...].astype(F32) + z1[...].astype(F32)

    def cell(f, r):
        return fields[f, r].astype(F32)

    def side(even, edge, own, recv_even, recv_odd):
        return jnp.where(edge, own, jnp.where(even, recv_even, recv_odd)).astype(F32)

    def diff_x(f, i, x, y):
        r = x * ny + y
        if x == 0:
            left = side(x_even, at_x == 0, fields[f, y], x1[i, y], x0[i, y])
        else:
            left = cell(f, r - ny)
        if x == nx - 1:
            right = side(x_even, at_x == sizes[0] - 1, fields[f, r], x0[i, y], x1[i, y])
        else:
            right = cell(f, r + ny)
        return right - left

    def diff_y(f, i, x, y):
        r = x * ny + y
        if y == 0:
            left = side(y_even, at_y == 0, fields[f, r], y1[i, x], y0[i, x])
        else:
            left = cell(f, r - 1)
        if y == ny - 1:
            right = side(y_even, at_y == sizes[1] - 1, fields[f, r], y0[i, x], y1[i, x])
        else:
            right = cell(f, r + 1)
        return right - left

    def diff_z(f, i, r):
        k = i * cells + r
        value = cell(f, r)
        ends = jnp.take_along_axis(
            edges, jnp.where(lane == LANES - 1, 2 * k + 1, 2 * k), axis=1
        )
        left = jnp.where(lane == 0, ends, pltpu.roll(value, 1, 1))
        right = jnp.where(lane == LANES - 1, ends, pltpu.roll(value, LANES - 1, 1))
        return right - left

    def put(c, value):
        high = value.astype(BF16)
        panel[0:snaps, c * LANES : (c + 1) * LANES] = high
        panel[snaps : 2 * snaps, c * LANES : (c + 1) * LANES] = (
            value - high.astype(F32)
        ).astype(BF16)

    for x in range(nx):
        for y in range(ny):
            r = x * ny + y
            dilatation = 0.5 * (diff_x(0, 0, x, y) + diff_y(1, 0, x, y) + diff_z(2, 0, r))
            put(r, dilatation)
            rx, ry, rz = diff_x(3, 1, x, y), diff_y(3, 1, x, y), diff_z(3, 1, r)
            put(cells + r, jnp.sqrt(0.25 * (rx * rx + ry * ry + rz * rz) + 0.25))

    def product(a, b):
        return lax.dot_general(a, b, (((1,), (1,)), ((), ())), preferred_element_type=F32)

    high, low = panel[0:snaps, :], panel[snaps : 2 * snaps, :]
    total = (product(high, high) + product(high, low) + product(low, high)) * scale
    moments[...] = fold(total)


def basis_kernel(
    dims, moments, panel, basis, factor, work, inverse, upper, columns, held, ready, sent
):
    snaps, nx, ny = dims
    cells = 2 * nx * ny
    copies = []

    def emit(first, final):
        count = final - first
        exact = inverse[first:final, 0:snaps]
        high = exact.astype(BF16)
        rest = (exact - high.astype(F32)).astype(BF16)
        left = jnp.concatenate(
            [
                jnp.concatenate([high, high], axis=1),
                jnp.concatenate([rest, jnp.zeros_like(rest)], axis=1),
            ],
            axis=0,
        )
        for c in range(0, cells, 2):
            both = jnp.dot(left, panel[:, c * LANES : (c + 2) * LANES], preferred_element_type=F32)
            out = both[0:count] + both[count : 2 * count]
            for i in range(2):
                ready[pl.ds(first * cells + c + i, count, stride=cells), :] = out[
                    :, i * LANES : (i + 1) * LANES
                ]
        part = pl.ds(first * cells, count * cells)
        copies.append(
            pltpu.make_async_copy(ready.at[part], basis.at[part], sent.at[len(copies)])
        )
        copies[-1].start()

    lane = lane_index(8)
    sub = lax.broadcasted_iota(jnp.int32, (8, LANES), 0)
    groups = snaps // 8
    unfold(moments[...], work)

    def spread(value, j):
        return jnp.take_along_axis(value, jnp.full((8, LANES), j, jnp.int32), axis=1)

    def column_set(base):
        block = work[base : base + 8, :]
        return block, [spread(block, base + i) for i in range(8)]

    def repeat(base, block, cols):
        work[base : base + 8, :] = block
        for i in range(8):
            columns[8 * (base + i) : 8 * (base + i) + 8, :] = cols[i]
        corner = [
            [columns[pl.ds(8 * (base + i) + j, 8, stride=0), :] for j in range(i + 1)]
            for i in range(8)
        ]
        return [work[pl.ds(base + i, 8, stride=0), :] for i in range(8)], corner

    rows, small = repeat(0, *column_set(0))
    for g in range(groups):
        base = 8 * g
        inside = (lane >= base) & (lane < base + 8)
        last = g + 1 == groups
        if not last:
            block, cols = column_set(base + 8)
            block = jnp.where(inside, 0.0, block)
        outer = []
        done = jnp.zeros((8, LANES), F32)
        roots = jnp.zeros((8, LANES), F32)
        for j in range(8):
            here = base + j
            root = lax.rsqrt(small[j][j])
            inv = root * root
            pivot = jnp.where(lane == here, 1.0, rows[j])
            for i in range(j + 1, 8):
                m = small[i][j] * inv
                rows[i] = jnp.where(lane == here, 0.0, rows[i]) - m * pivot
                for k in range(j + 1, i + 1):
                    small[i][k] = small[i][k] - m * small[k][j]
            done = jnp.where(sub == j, rows[j] * root, done)
            roots = jnp.where(sub == j, root, roots)
            if last:
                continue
            clean = jnp.where((lane > here) & (lane < base + 8), 0.0, pivot) * inv
            outer.append(clean)
            m = jnp.take_along_axis(rows[j], sub + base + 8, axis=1)
            held[8 * here : 8 * here + 8, :] = m
            block = block - m * clean
            m = m * inv
            for i in range(8):
                cols[i] = cols[i] - m * held[pl.ds(8 * here + i, 8, stride=0), :]
        upper[base : base + 8, :] = jnp.where(lane >= sub + base, done, 0.0)[:, 0:snaps]
        inverse[base : base + 8, :] = jnp.where(
            lane < sub + base, done, jnp.where(lane == sub + base, roots, 0.0)
        )
        if last:
            break
        if base + 8 in CUTS:
            emit(CUTS[CUTS.index(base + 8) - 1], base + 8)
        rows_next, small = repeat(base + 8, block, cols)
        for h in range(g + 2, groups):
            block = jnp.where(inside, 0.0, work[8 * h : 8 * h + 8, :])
            for j in range(8):
                m = jnp.take_along_axis(rows[j], sub + 8 * h, axis=1)
                block = block - m * outer[j]
            work[8 * h : 8 * h + 8, :] = block
        rows = rows_next
    copies.append(pltpu.make_async_copy(upper, factor, sent.at[len(copies)]))
    copies[-1].start()
    emit(CUTS[-1], snaps)
    for copy in copies:
        copy.wait()


def per_device(mate, vel_u, vel_v, vel_w, density):
    snaps, nx, ny, nz = vel_u.shape
    cells = nx * ny
    dims = (snaps, nx, ny)
    sizes = tuple(lax.axis_size(a) for a in AXES)
    flat = [
        pltpu.with_memory_space_constraint(a.reshape(snaps * cells, nz), pltpu.HBM)
        for a in (vel_u, vel_v, vel_w, density)
    ]
    params = pltpu.CompilerParams(vmem_limit_bytes=48 << 20)
    x_face = jax.ShapeDtypeStruct((2, ny, snaps, nz), BF16)
    y_face = jax.ShapeDtypeStruct((2, nx, snaps, nz), BF16)
    z_face = jax.ShapeDtypeStruct((snaps, nz), BF16)
    fields, x0, x1, y0, y1, z0, z1 = pl.pallas_call(
        functools.partial(pack_kernel, dims),
        out_shape=(
            jax.ShapeDtypeStruct((4, cells, snaps, nz), BF16),
            x_face,
            x_face,
            y_face,
            y_face,
            z_face,
            z_face,
        ),
        in_specs=[HBM] * 4,
        out_specs=[VMEM] * 7,
        scratch_shapes=[
            pltpu.VMEM((4, snaps * cells, nz), BF16),
            pltpu.VMEM((4, snaps * cells, nz), F32),
            pltpu.SemaphoreType.DMA((4,)),
        ],
        compiler_params=params,
        name="pack",
    )(*flat)
    x0 = swapped(x0, "gx", 0)
    y0 = swapped(y0, "gy", 0)
    if sizes[1] > 2:
        y1 = swapped(y1, "gy", 1)
    z0 = swapped(z0, "gz", 0)
    z1 = swapped(z1, "gz", 1, True)
    if sizes[0] > 2:
        x1 = swapped(x1, "gx", 1)
    scale = 1.0 / (2 * cells * nz * sizes[0] * sizes[1] * sizes[2])
    panel, moments = pl.pallas_call(
        functools.partial(panel_kernel, dims, scale, sizes),
        out_shape=(
            jax.ShapeDtypeStruct((2 * snaps, 2 * cells * nz), BF16),
            jax.ShapeDtypeStruct((snaps // 2, LANES), F32),
        ),
        in_specs=[VMEM] * 7,
        out_specs=[VMEM] * 2,
        compiler_params=params,
        name="panel",
    )(fields, x0, x1, y0, y1, z0, z1)
    moments = summed(moments, mate)
    basis, factor = pl.pallas_call(
        functools.partial(basis_kernel, dims),
        out_shape=(
            jax.ShapeDtypeStruct((snaps * 2 * cells, nz), F32),
            jax.ShapeDtypeStruct((snaps, snaps), F32),
        ),
        in_specs=[VMEM] * 2,
        out_specs=[HBM, HBM],
        scratch_shapes=[
            pltpu.VMEM((snaps, LANES), F32),
            pltpu.VMEM((snaps, LANES), F32),
            pltpu.VMEM((snaps, snaps), F32),
            pltpu.VMEM((8 * snaps, LANES), F32),
            pltpu.VMEM((8 * snaps, LANES), F32),
            pltpu.VMEM((snaps * 2 * cells, nz), F32),
            pltpu.SemaphoreType.DMA((len(CUTS) + 1,)),
        ],
        compiler_params=params,
        name="basis",
    )(moments, panel)
    return basis.reshape(snaps, 2, nx, ny, nz), factor


def chip_mate(mesh):
    devices = list(mesh.devices.flat)
    at = [getattr(d, "coords", None) for d in devices]
    near = [k for k in range(1, len(at)) if at[0] is not None and at[k] == at[0]]
    return near[0] if near and near[0] & (near[0] - 1) == 0 else 1


def solution(mesh):
    spec = P(None, "gx", "gy", "gz")
    return jax.shard_map(
        functools.partial(per_device, chip_mate(mesh)),
        mesh=mesh,
        in_specs=(spec,) * 4,
        out_specs=(P(None, None, "gx", "gy", "gz"), P()),
        check_vma=False,
    )
```

```python
import functools

import jax
import jax.numpy as jnp
import numpy as np
from jax import lax
from jax.experimental import pallas as pl
from jax.experimental.pallas import tpu as pltpu
from jax.sharding import PartitionSpec as P

F32 = jnp.float32
BF16 = jnp.bfloat16
LANES = 128
CUTS = (0, 64)
VMEM = pl.BlockSpec(memory_space=pltpu.VMEM)
HBM = pl.BlockSpec(memory_space=pltpu.HBM)


AXES = ("gx", "gy", "gz")


def swapped(value, axis, first, periodic=False):
    sizes = [lax.axis_size(a) for a in AXES]
    where = AXES.index(axis)
    count = sizes[where]
    out = []
    for here in np.ndindex(*sizes):
        to = list(here)
        to[where] += 1 if here[where] % 2 == first else -1
        if periodic:
            to[where] %= count
        if not 0 <= to[where] < count:
            to = [here[0], here[1], here[2] ^ 1]
        out.append((int(np.ravel_multi_index(here, sizes)), int(np.ravel_multi_index(to, sizes))))
    return lax.ppermute(value, AXES, out)


def summed(value, mate):
    count = int(np.prod([lax.axis_size(a) for a in AXES]))
    if count & (count - 1):
        return lax.psum(value, AXES)
    steps = [mate] + [
        1 << k | mate for k in range(count.bit_length() - 1) if 1 << k != mate
    ]
    for step in steps:
        value = value + lax.ppermute(value, AXES, [(i, i ^ step) for i in range(count)])
    return value


def lane_index(rows):
    return lax.broadcasted_iota(jnp.int32, (rows, LANES), 1)


def fold(full):
    full = jnp.concatenate([full, jnp.zeros((96, LANES - 96), F32)], axis=1)
    top, rest = full[0:48], full[48:96]
    lane = lane_index(48)
    near = pltpu.roll(rest, 48, 1)
    far = pltpu.roll(rest, 64, 1)
    top = jnp.where(lane >= 96, near, top)
    lane = lane_index(16)
    middle = jnp.where(lane < 16, near[32:48], top[16:32])
    bottom = jnp.where(lane < 16, near[0:16], jnp.where(lane < 32, far[16:32], top[32:48]))
    return jnp.concatenate([top[0:16], middle, bottom], axis=0)


def unfold(folded, work):
    lane = lane_index(16)
    near = pltpu.roll(folded, 80, 1)
    far = pltpu.roll(folded[32:48], 64, 1)
    work[0:48, :] = folded
    work[48:64, :] = jnp.where(lane < 80, near[0:16], near[32:48])
    work[64:80, :] = jnp.where(lane < 80, near[16:32], far)
    work[80:96, :] = jnp.where(lane < 80, near[32:48], near[16:32])


def row_of(wide, dims, f, r):
    return wide[f, pl.ds(r, dims[0], stride=dims[1] * dims[2]), :]


def sent_row(dims, f, r):
    x, y = divmod(r, dims[2])
    return f >= 2 or (x if f == 0 else y) in (0, dims[1 + f] - 1)


def pack_kernel(
    dims, u, v, w, rho, fields, wide, x0, x1, y0, y1, z0, z1, narrow, extra, arrived
):
    snaps, nx, ny = dims
    cells = nx * ny
    copies = [
        pltpu.make_async_copy(ref, narrow.at[f], arrived.at[f])
        for f, ref in enumerate((u, v, w, rho))
    ]
    for copy in copies:
        copy.start()
    x_even = lax.axis_index("gx") % 2 == 0
    y_even = lax.axis_index("gy") % 2 == 0
    z_even = lax.axis_index("gz") % 2 == 0
    lane = lane_index(snaps)
    column = jnp.zeros((snaps, LANES), F32)
    for f in range(4):
        copies[f].wait()
        from_rows = functools.partial(row_of, wide if f < 2 else extra, dims, f % 2)
        if f < 2:
            wide[f] = narrow[f].astype(F32)
        else:
            extra[f - 2] = narrow[f].astype(F32)
        for r in range(cells):
            if not sent_row(dims, f, r):
                continue
            value = from_rows(r)
            fields[f, r] = value
            if f >= 2:
                k = (f - 2) * cells + r
                moved = pltpu.roll(value, 2 * k + 1, 1)
                column = jnp.where((lane == 2 * k) | (lane == 2 * k + 1), moved, column)
        if f in (0, 3):
            for y in range(ny):
                first, final = fields[f, y], fields[f, (nx - 1) * ny + y]
                x0[f // 3, y] = jnp.where(x_even, final, first).astype(BF16)
                x1[f // 3, y] = jnp.where(x_even, first, final).astype(BF16)
        if f in (1, 3):
            for x in range(nx):
                first, final = fields[f, x * ny], fields[f, x * ny + ny - 1]
                y0[f // 3, x] = jnp.where(y_even, final, first).astype(BF16)
                y1[f // 3, x] = jnp.where(y_even, first, final).astype(BF16)
    final = jnp.where(lane % 2 == 0, column, 0.0)
    first = jnp.where(lane % 2 == 1, column, 0.0)
    z0[...] = jnp.where(z_even, final, first).astype(BF16)
    z1[...] = jnp.where(z_even, first, final).astype(BF16)


def inner_kernel(dims, fields, wide, inner, select):
    snaps, nx, ny = dims
    cells = nx * ny
    lane = lane_index(snaps)

    def row(f, r):
        return fields[f, r] if sent_row(dims, f, r) else row_of(wide, dims, f, r)

    sub = lax.broadcasted_iota(jnp.int32, (LANES, LANES), 0)
    at = lane_index(LANES)
    first, final = at == 0, at == LANES - 1
    for k in range(2 * cells):
        low = jnp.where(first & (sub == 2 * k), -1.0, 0.0)
        both = jnp.where(final & (sub == 2 * k + 1), 1.0, low)
        select[:, k * LANES : (k + 1) * LANES] = both.astype(BF16)

    def along(f, position, count, low, high):
        if position == 0:
            return row(f, high)
        if position == count - 1:
            return -row(f, low)
        return row(f, high) - row(f, low)

    def across(f, r):
        value = row(f, r)
        right = jnp.where(lane == LANES - 1, 0.0, pltpu.roll(value, LANES - 1, 1))
        return right - jnp.where(lane == 0, 0.0, pltpu.roll(value, 1, 1))

    for x in range(nx):
        for y in range(ny):
            r = x * ny + y
            inner[0, r] = (
                along(0, x, nx, r - ny, r + ny) + along(1, y, ny, r - 1, r + 1) + across(2, r)
            )
            inner[1, r] = along(3, x, nx, r - ny, r + ny)
            inner[2, r] = along(3, y, ny, r - 1, r + 1)
            inner[3, r] = across(3, r)


def panel_kernel(
    dims, scale, sizes, fields, inner, select, x0, x1, y0, y1, z0, z1, panel, moments
):
    snaps, nx, ny = dims
    cells = nx * ny
    at_x, at_y = lax.axis_index("gx"), lax.axis_index("gy")
    x_even, y_even = at_x % 2 == 0, at_y % 2 == 0
    edges = (z0[...].astype(F32) + z1[...].astype(F32)).astype(BF16)

    def outside(f, r, edge, received):
        return jnp.where(edge, fields[f, r], received.astype(F32))

    def add_x(value, f, i, x, y):
        if x == 0:
            received = jnp.where(x_even, x1[i, y], x0[i, y])
            value = value - outside(f, x * ny + y, at_x == 0, received)
        if x == nx - 1:
            received = jnp.where(x_even, x0[i, y], x1[i, y])
            value = value + outside(f, x * ny + y, at_x == sizes[0] - 1, received)
        return value

    def add_y(value, f, i, x, y):
        if y == 0:
            received = jnp.where(y_even, y1[i, x], y0[i, x])
            value = value - outside(f, x * ny + y, at_y == 0, received)
        if y == ny - 1:
            received = jnp.where(y_even, y0[i, x], y1[i, x])
            value = value + outside(f, x * ny + y, at_y == sizes[1] - 1, received)
        return value

    def add_z(value, i, r):
        k = i * cells + r
        near = jnp.dot(
            edges, select[:, k * LANES : (k + 1) * LANES], preferred_element_type=F32
        )
        return value + near

    def put(c, value):
        high = value.astype(BF16)
        panel[0:snaps, c * LANES : (c + 1) * LANES] = high
        panel[snaps : 2 * snaps, c * LANES : (c + 1) * LANES] = (
            value - high.astype(F32)
        ).astype(BF16)

    for x in range(nx):
        for y in range(ny):
            r = x * ny + y
            total = add_y(add_x(inner[0, r], 0, 0, x, y), 1, 0, x, y)
            put(r, 0.5 * add_z(total, 0, r))
            rx = add_x(inner[1, r], 3, 1, x, y)
            ry = add_y(inner[2, r], 3, 1, x, y)
            rz = add_z(inner[3, r], 1, r)
            put(cells + r, jnp.sqrt(0.25 * (rx * rx + ry * ry + rz * rz) + 0.25))

    def product(a, b):
        return lax.dot_general(a, b, (((1,), (1,)), ((), ())), preferred_element_type=F32)

    both = product(panel[...], panel[0:snaps, :])
    cross = both[snaps : 2 * snaps]
    total = (both[0:snaps] + cross + cross.T) * scale
    moments[...] = fold(total)


def basis_kernel(
    dims, moments, panel, basis, factor, work, inverse, upper, columns, held, ready, sent
):
    snaps, nx, ny = dims
    cells = 2 * nx * ny
    copies = []

    def emit(first, final):
        count = final - first
        exact = inverse[first:final, 0:snaps]
        high = exact.astype(BF16)
        rest = (exact - high.astype(F32)).astype(BF16)
        left = jnp.concatenate(
            [
                jnp.concatenate([high, high], axis=1),
                jnp.concatenate([rest, jnp.zeros_like(rest)], axis=1),
            ],
            axis=0,
        )
        for c in range(0, cells, 2):
            both = jnp.dot(left, panel[:, c * LANES : (c + 2) * LANES], preferred_element_type=F32)
            out = both[0:count] + both[count : 2 * count]
            for i in range(2):
                ready[pl.ds(first * cells + c + i, count, stride=cells), :] = out[
                    :, i * LANES : (i + 1) * LANES
                ]
        part = pl.ds(first * cells, count * cells)
        copies.append(
            pltpu.make_async_copy(ready.at[part], basis.at[part], sent.at[len(copies)])
        )
        copies[-1].start()

    lane = lane_index(8)
    sub = lax.broadcasted_iota(jnp.int32, (8, LANES), 0)
    groups = snaps // 8
    unfold(moments[...], work)

    def spread(value, j):
        return jnp.take_along_axis(value, jnp.full((8, LANES), j, jnp.int32), axis=1)

    def column_set(base):
        block = work[base : base + 8, :]
        return block, [spread(block, base + i) for i in range(8)]

    def repeat(base, block, cols):
        work[base : base + 8, :] = block
        for i in range(8):
            columns[8 * (base + i) : 8 * (base + i) + 8, :] = cols[i]
        corner = [
            [columns[pl.ds(8 * (base + i) + j, 8, stride=0), :] for j in range(i + 1)]
            for i in range(8)
        ]
        return [work[pl.ds(base + i, 8, stride=0), :] for i in range(8)], corner

    rows, small = repeat(0, *column_set(0))
    for g in range(groups):
        base = 8 * g
        inside = (lane >= base) & (lane < base + 8)
        last = g + 1 == groups
        if not last:
            block, cols = column_set(base + 8)
            block = jnp.where(inside, 0.0, block)
        outer = []
        done = jnp.zeros((8, LANES), F32)
        roots = jnp.zeros((8, LANES), F32)
        for j in range(8):
            here = base + j
            root = lax.rsqrt(small[j][j])
            inv = root * root
            pivot = jnp.where(lane == here, 1.0, rows[j])
            for i in range(j + 1, 8):
                m = small[i][j] * inv
                rows[i] = jnp.where(lane == here, 0.0, rows[i]) - m * pivot
                for k in range(j + 1, i + 1):
                    small[i][k] = small[i][k] - m * small[k][j]
            done = jnp.where(sub == j, rows[j] * root, done)
            roots = jnp.where(sub == j, root, roots)
            if last:
                continue
            clean = jnp.where((lane > here) & (lane < base + 8), 0.0, pivot) * inv
            outer.append(clean)
            m = jnp.take_along_axis(rows[j], sub + base + 8, axis=1)
            held[8 * here : 8 * here + 8, :] = m
            block = block - m * clean
            m = m * inv
            for i in range(8):
                cols[i] = cols[i] - m * held[pl.ds(8 * here + i, 8, stride=0), :]
        upper[base : base + 8, :] = jnp.where(lane >= sub + base, done, 0.0)[:, 0:snaps]
        inverse[base : base + 8, :] = jnp.where(
            lane < sub + base, done, jnp.where(lane == sub + base, roots, 0.0)
        )
        if last:
            break
        if base + 8 in CUTS:
            emit(CUTS[CUTS.index(base + 8) - 1], base + 8)
        rows_next, small = repeat(base + 8, block, cols)
        for h in range(g + 2, groups):
            block = jnp.where(inside, 0.0, work[8 * h : 8 * h + 8, :])
            for j in range(8):
                m = jnp.take_along_axis(rows[j], sub + 8 * h, axis=1)
                block = block - m * outer[j]
            work[8 * h : 8 * h + 8, :] = block
        rows = rows_next
    copies.append(pltpu.make_async_copy(upper, factor, sent.at[len(copies)]))
    copies[-1].start()
    emit(CUTS[-1], snaps)
    for copy in copies:
        copy.wait()


def per_device(mate, vel_u, vel_v, vel_w, density):
    snaps, nx, ny, nz = vel_u.shape
    cells = nx * ny
    dims = (snaps, nx, ny)
    sizes = tuple(lax.axis_size(a) for a in AXES)
    flat = [
        pltpu.with_memory_space_constraint(a.reshape(snaps * cells, nz), pltpu.HBM)
        for a in (vel_u, vel_v, vel_w, density)
    ]
    params = pltpu.CompilerParams(vmem_limit_bytes=12 << 20)
    x_face = jax.ShapeDtypeStruct((2, ny, snaps, nz), BF16)
    y_face = jax.ShapeDtypeStruct((2, nx, snaps, nz), BF16)
    z_face = jax.ShapeDtypeStruct((snaps, nz), BF16)
    fields, wide, x0, x1, y0, y1, z0, z1 = pl.pallas_call(
        functools.partial(pack_kernel, dims),
        out_shape=(
            jax.ShapeDtypeStruct((4, cells, snaps, nz), F32),
            jax.ShapeDtypeStruct((2, snaps * cells, nz), F32),
            x_face,
            x_face,
            y_face,
            y_face,
            z_face,
            z_face,
        ),
        in_specs=[HBM] * 4,
        out_specs=[VMEM] * 8,
        scratch_shapes=[
            pltpu.VMEM((4, snaps * cells, nz), BF16),
            pltpu.VMEM((2, snaps * cells, nz), F32),
            pltpu.SemaphoreType.DMA((4,)),
        ],
        compiler_params=params,
        name="pack",
    )(*flat)
    x0 = swapped(x0, "gx", 0)
    y0 = swapped(y0, "gy", 0)
    if sizes[1] > 2:
        y1 = swapped(y1, "gy", 1)
    z0 = swapped(z0, "gz", 0)
    z1 = swapped(z1, "gz", 1, True)
    if sizes[0] > 2:
        x1 = swapped(x1, "gx", 1)
    inner, select = pl.pallas_call(
        functools.partial(inner_kernel, dims),
        out_shape=(
            jax.ShapeDtypeStruct((4, cells, snaps, nz), F32),
            jax.ShapeDtypeStruct((nz, 2 * cells * nz), BF16),
        ),
        in_specs=[VMEM] * 2,
        out_specs=[VMEM] * 2,
        compiler_params=params,
        name="inner",
    )(fields, wide)
    scale = 1.0 / (2 * cells * nz * sizes[0] * sizes[1] * sizes[2])
    panel, moments = pl.pallas_call(
        functools.partial(panel_kernel, dims, scale, sizes),
        out_shape=(
            jax.ShapeDtypeStruct((2 * snaps, 2 * cells * nz), BF16),
            jax.ShapeDtypeStruct((snaps // 2, LANES), F32),
        ),
        in_specs=[VMEM] * 9,
        out_specs=[VMEM] * 2,
        compiler_params=params,
        name="panel",
    )(fields, inner, select, x0, x1, y0, y1, z0, z1)
    moments = summed(moments, mate)
    basis, factor = pl.pallas_call(
        functools.partial(basis_kernel, dims),
        out_shape=(
            jax.ShapeDtypeStruct((snaps * 2 * cells, nz), F32),
            jax.ShapeDtypeStruct((snaps, snaps), F32),
        ),
        in_specs=[VMEM] * 2,
        out_specs=[HBM, HBM],
        scratch_shapes=[
            pltpu.VMEM((snaps, LANES), F32),
            pltpu.VMEM((snaps, LANES), F32),
            pltpu.VMEM((snaps, snaps), F32),
            pltpu.VMEM((8 * snaps, LANES), F32),
            pltpu.VMEM((8 * snaps, LANES), F32),
            pltpu.VMEM((snaps * 2 * cells, nz), F32),
            pltpu.SemaphoreType.DMA((len(CUTS) + 1,)),
        ],
        compiler_params=params,
        name="basis",
    )(moments, panel)
    return basis.reshape(snaps, 2, nx, ny, nz), factor


def chip_mate(mesh):
    devices = list(mesh.devices.flat)
    at = [getattr(d, "coords", None) for d in devices]
    near = [k for k in range(1, len(at)) if at[0] is not None and at[k] == at[0]]
    return near[0] if near and near[0] & (near[0] - 1) == 0 else 1


def solution(mesh):
    spec = P(None, "gx", "gy", "gz")
    return jax.shard_map(
        functools.partial(per_device, chip_mate(mesh)),
        mesh=mesh,
        in_specs=(spec,) * 4,
        out_specs=(P(None, None, "gx", "gy", "gz"), P()),
        check_vma=False,
    )
```

```python
import functools

import jax
import jax.numpy as jnp
import numpy as np
from jax import lax
from jax.experimental import pallas as pl
from jax.experimental.pallas import tpu as pltpu
from jax.sharding import PartitionSpec as P

F32 = jnp.float32
BF16 = jnp.bfloat16
LANES = 128
CUTS = (0, 64)
VMEM = pl.BlockSpec(memory_space=pltpu.VMEM)
HBM = pl.BlockSpec(memory_space=pltpu.HBM)


AXES = ("gx", "gy", "gz")


def swapped(value, axis, first, periodic=False):
    sizes = [lax.axis_size(a) for a in AXES]
    where = AXES.index(axis)
    count = sizes[where]
    out = []
    for here in np.ndindex(*sizes):
        to = list(here)
        to[where] += 1 if here[where] % 2 == first else -1
        if periodic:
            to[where] %= count
        if not 0 <= to[where] < count:
            to = [here[0], here[1], here[2] ^ 1]
        out.append((int(np.ravel_multi_index(here, sizes)), int(np.ravel_multi_index(to, sizes))))
    return lax.ppermute(value, AXES, out)


def summed(value, mate):
    sizes = [lax.axis_size(a) for a in AXES]
    count = int(np.prod(sizes))
    if count & (count - 1):
        return lax.psum(value, AXES)

    def other(step):
        return lax.ppermute(value, AXES, [(i, i ^ step) for i in range(count)])

    steps = [1 << k for k in reversed(range(count.bit_length() - 1)) if 1 << k != mate]
    last = [k for k in (count // 2, sizes[2]) if k in steps]
    if len(set(last)) < 2:
        last = steps[:2]
    value = value + other(mate)
    for step in steps:
        if step not in last:
            value = value + other(step | mate)
    if len(last) < 2:
        return value + other(last[0] | mate) if last else value
    one, two, both = other(last[0] | mate), other(last[1] | mate), other(sum(last) | mate)
    return (value + one) + (two + both)


def lane_index(rows):
    return lax.broadcasted_iota(jnp.int32, (rows, LANES), 1)


def fold(full):
    full = jnp.concatenate([full, jnp.zeros((96, LANES - 96), F32)], axis=1)
    top, rest = full[0:48], full[48:96]
    lane = lane_index(48)
    near = pltpu.roll(rest, 48, 1)
    far = pltpu.roll(rest, 64, 1)
    top = jnp.where(lane >= 96, near, top)
    lane = lane_index(16)
    middle = jnp.where(lane < 16, near[32:48], top[16:32])
    bottom = jnp.where(lane < 16, near[0:16], jnp.where(lane < 32, far[16:32], top[32:48]))
    return jnp.concatenate([top[0:16], middle, bottom], axis=0)


def unfold(folded, work):
    lane = lane_index(16)
    near = pltpu.roll(folded, 80, 1)
    far = pltpu.roll(folded[32:48], 64, 1)
    work[0:48, :] = folded
    work[48:64, :] = jnp.where(lane < 80, near[0:16], near[32:48])
    work[64:80, :] = jnp.where(lane < 80, near[16:32], far)
    work[80:96, :] = jnp.where(lane < 80, near[32:48], near[16:32])


def row_of(wide, dims, f, r):
    return wide[f, pl.ds(r, dims[0], stride=dims[1] * dims[2]), :]


def sent_row(dims, f, r):
    x, y = divmod(r, dims[2])
    return f >= 2 or (x if f == 0 else y) in (0, dims[1 + f] - 1)


def pack_kernel(
    dims, u, v, w, rho, fields, wide, x0, x1, y0, y1, z0, z1, narrow, extra, arrived
):
    snaps, nx, ny = dims
    cells = nx * ny
    copies = [
        pltpu.make_async_copy(ref, narrow.at[f], arrived.at[f])
        for f, ref in enumerate((u, v, w, rho))
    ]
    for copy in copies:
        copy.start()
    x_even = lax.axis_index("gx") % 2 == 0
    y_even = lax.axis_index("gy") % 2 == 0
    z_even = lax.axis_index("gz") % 2 == 0
    lane = lane_index(snaps)
    column = jnp.zeros((snaps, LANES), F32)
    for f in range(4):
        copies[f].wait()
        from_rows = functools.partial(row_of, wide if f < 2 else extra, dims, f % 2)
        if f < 2:
            wide[f] = narrow[f].astype(F32)
        else:
            extra[f - 2] = narrow[f].astype(F32)
        for r in range(cells):
            if not sent_row(dims, f, r):
                continue
            value = from_rows(r)
            fields[f, r] = value
            if f >= 2:
                k = (f - 2) * cells + r
                moved = pltpu.roll(value, 2 * k + 1, 1)
                column = jnp.where((lane == 2 * k) | (lane == 2 * k + 1), moved, column)
        if f in (0, 3):
            for y in range(ny):
                first, final = fields[f, y], fields[f, (nx - 1) * ny + y]
                x0[f // 3, y] = jnp.where(x_even, final, first).astype(BF16)
                x1[f // 3, y] = jnp.where(x_even, first, final).astype(BF16)
        if f in (1, 3):
            for x in range(nx):
                first, final = fields[f, x * ny], fields[f, x * ny + ny - 1]
                y0[f // 3, x] = jnp.where(y_even, final, first).astype(BF16)
                y1[f // 3, x] = jnp.where(y_even, first, final).astype(BF16)
    final = jnp.where(lane % 2 == 0, column, 0.0)
    first = jnp.where(lane % 2 == 1, column, 0.0)
    z0[...] = jnp.where(z_even, final, first).astype(BF16)
    z1[...] = jnp.where(z_even, first, final).astype(BF16)


def inner_kernel(dims, fields, wide, inner, select):
    snaps, nx, ny = dims
    cells = nx * ny
    lane = lane_index(snaps)

    def row(f, r):
        return fields[f, r] if sent_row(dims, f, r) else row_of(wide, dims, f, r)

    sub = lax.broadcasted_iota(jnp.int32, (LANES, LANES), 0)
    at = lane_index(LANES)
    first, final = at == 0, at == LANES - 1
    for k in range(2 * cells):
        low = jnp.where(first & (sub == 2 * k), -1.0, 0.0)
        both = jnp.where(final & (sub == 2 * k + 1), 1.0, low)
        select[:, k * LANES : (k + 1) * LANES] = both.astype(BF16)

    def along(f, position, count, low, high):
        if position == 0:
            return row(f, high)
        if position == count - 1:
            return -row(f, low)
        return row(f, high) - row(f, low)

    def across(f, r):
        value = row(f, r)
        right = jnp.where(lane == LANES - 1, 0.0, pltpu.roll(value, LANES - 1, 1))
        return right - jnp.where(lane == 0, 0.0, pltpu.roll(value, 1, 1))

    for x in range(nx):
        for y in range(ny):
            r = x * ny + y
            inner[0, r] = (
                along(0, x, nx, r - ny, r + ny) + along(1, y, ny, r - 1, r + 1) + across(2, r)
            )
            inner[1, r] = along(3, x, nx, r - ny, r + ny)
            inner[2, r] = along(3, y, ny, r - 1, r + 1)
            inner[3, r] = across(3, r)


def panel_kernel(
    dims, scale, sizes, fields, inner, select, x0, x1, y0, y1, z0, z1, panel, moments
):
    snaps, nx, ny = dims
    cells = nx * ny
    at_x, at_y = lax.axis_index("gx"), lax.axis_index("gy")
    x_even, y_even = at_x % 2 == 0, at_y % 2 == 0
    edges = (z0[...].astype(F32) + z1[...].astype(F32)).astype(BF16)

    def outside(f, r, edge, received):
        return jnp.where(edge, fields[f, r], received.astype(F32))

    def add_x(value, f, i, x, y):
        if x == 0:
            received = jnp.where(x_even, x1[i, y], x0[i, y])
            value = value - outside(f, x * ny + y, at_x == 0, received)
        if x == nx - 1:
            received = jnp.where(x_even, x0[i, y], x1[i, y])
            value = value + outside(f, x * ny + y, at_x == sizes[0] - 1, received)
        return value

    def add_y(value, f, i, x, y):
        if y == 0:
            received = jnp.where(y_even, y1[i, x], y0[i, x])
            value = value - outside(f, x * ny + y, at_y == 0, received)
        if y == ny - 1:
            received = jnp.where(y_even, y0[i, x], y1[i, x])
            value = value + outside(f, x * ny + y, at_y == sizes[1] - 1, received)
        return value

    def add_z(value, i, r):
        k = i * cells + r
        near = jnp.dot(
            edges, select[:, k * LANES : (k + 1) * LANES], preferred_element_type=F32
        )
        return value + near

    def put(c, value):
        high = value.astype(BF16)
        panel[0:snaps, c * LANES : (c + 1) * LANES] = high
        panel[snaps : 2 * snaps, c * LANES : (c + 1) * LANES] = (
            value - high.astype(F32)
        ).astype(BF16)

    for x in range(nx):
        for y in range(ny):
            r = x * ny + y
            total = add_y(add_x(inner[0, r], 0, 0, x, y), 1, 0, x, y)
            put(r, 0.5 * add_z(total, 0, r))
            rx = add_x(inner[1, r], 3, 1, x, y)
            ry = add_y(inner[2, r], 3, 1, x, y)
            rz = add_z(inner[3, r], 1, r)
            put(cells + r, jnp.sqrt(0.25 * (rx * rx + ry * ry + rz * rz) + 0.25))

    def product(a, b):
        return lax.dot_general(a, b, (((1,), (1,)), ((), ())), preferred_element_type=F32)

    both = product(panel[...], panel[0:snaps, :])
    cross = both[snaps : 2 * snaps]
    total = (both[0:snaps] + cross + cross.T) * scale
    moments[...] = fold(total)


def basis_kernel(
    dims, moments, panel, basis, factor, work, inverse, upper, columns, held, ready, sent
):
    snaps, nx, ny = dims
    cells = 2 * nx * ny
    copies = []

    def emit(first, final):
        count = final - first
        exact = inverse[first:final, 0:snaps]
        high = exact.astype(BF16)
        rest = (exact - high.astype(F32)).astype(BF16)
        left = jnp.concatenate(
            [
                jnp.concatenate([high, high], axis=1),
                jnp.concatenate([rest, jnp.zeros_like(rest)], axis=1),
            ],
            axis=0,
        )
        for c in range(0, cells, 2):
            both = jnp.dot(left, panel[:, c * LANES : (c + 2) * LANES], preferred_element_type=F32)
            out = both[0:count] + both[count : 2 * count]
            for i in range(2):
                ready[pl.ds(first * cells + c + i, count, stride=cells), :] = out[
                    :, i * LANES : (i + 1) * LANES
                ]
        part = pl.ds(first * cells, count * cells)
        copies.append(
            pltpu.make_async_copy(ready.at[part], basis.at[part], sent.at[len(copies)])
        )
        copies[-1].start()

    lane = lane_index(8)
    sub = lax.broadcasted_iota(jnp.int32, (8, LANES), 0)
    groups = snaps // 8
    unfold(moments[...], work)

    def spread(value, j):
        return jnp.take_along_axis(value, jnp.full((8, LANES), j, jnp.int32), axis=1)

    def column_set(base):
        block = work[base : base + 8, :]
        return block, [spread(block, base + i) for i in range(8)]

    def repeat(base, block, cols):
        work[base : base + 8, :] = block
        for i in range(8):
            columns[8 * (base + i) : 8 * (base + i) + 8, :] = cols[i]
        corner = [
            [columns[pl.ds(8 * (base + i) + j, 8, stride=0), :] for j in range(i + 1)]
            for i in range(8)
        ]
        return [work[pl.ds(base + i, 8, stride=0), :] for i in range(8)], corner

    rows, small = repeat(0, *column_set(0))
    for g in range(groups):
        base = 8 * g
        inside = (lane >= base) & (lane < base + 8)
        last = g + 1 == groups
        if not last:
            block, cols = column_set(base + 8)
            block = jnp.where(inside, 0.0, block)
        outer = []
        done = jnp.zeros((8, LANES), F32)
        roots = jnp.zeros((8, LANES), F32)
        for j in range(8):
            here = base + j
            root = lax.rsqrt(small[j][j])
            inv = root * root
            pivot = jnp.where(lane == here, 1.0, rows[j])
            for i in range(j + 1, 8):
                m = small[i][j] * inv
                rows[i] = jnp.where(lane == here, 0.0, rows[i]) - m * pivot
                for k in range(j + 1, i + 1):
                    small[i][k] = small[i][k] - m * small[k][j]
            done = jnp.where(sub == j, rows[j] * root, done)
            roots = jnp.where(sub == j, root, roots)
            if last:
                continue
            clean = jnp.where((lane > here) & (lane < base + 8), 0.0, pivot) * inv
            outer.append(clean)
            m = jnp.take_along_axis(rows[j], sub + base + 8, axis=1)
            held[8 * here : 8 * here + 8, :] = m
            block = block - m * clean
            m = m * inv
            for i in range(8):
                cols[i] = cols[i] - m * held[pl.ds(8 * here + i, 8, stride=0), :]
        upper[base : base + 8, :] = jnp.where(lane >= sub + base, done, 0.0)[:, 0:snaps]
        inverse[base : base + 8, :] = jnp.where(
            lane < sub + base, done, jnp.where(lane == sub + base, roots, 0.0)
        )
        if last:
            break
        if base + 8 in CUTS:
            emit(CUTS[CUTS.index(base + 8) - 1], base + 8)
        rows_next, small = repeat(base + 8, block, cols)
        for h in range(g + 2, groups):
            block = jnp.where(inside, 0.0, work[8 * h : 8 * h + 8, :])
            for j in range(8):
                m = jnp.take_along_axis(rows[j], sub + 8 * h, axis=1)
                block = block - m * outer[j]
            work[8 * h : 8 * h + 8, :] = block
        rows = rows_next
    copies.append(pltpu.make_async_copy(upper, factor, sent.at[len(copies)]))
    copies[-1].start()
    emit(CUTS[-1], snaps)
    for copy in copies:
        copy.wait()


def per_device(mate, vel_u, vel_v, vel_w, density):
    snaps, nx, ny, nz = vel_u.shape
    cells = nx * ny
    dims = (snaps, nx, ny)
    sizes = tuple(lax.axis_size(a) for a in AXES)
    flat = [
        pltpu.with_memory_space_constraint(a.reshape(snaps * cells, nz), pltpu.HBM)
        for a in (vel_u, vel_v, vel_w, density)
    ]
    params = pltpu.CompilerParams(vmem_limit_bytes=12 << 20)
    x_face = jax.ShapeDtypeStruct((2, ny, snaps, nz), BF16)
    y_face = jax.ShapeDtypeStruct((2, nx, snaps, nz), BF16)
    z_face = jax.ShapeDtypeStruct((snaps, nz), BF16)
    fields, wide, x0, x1, y0, y1, z0, z1 = pl.pallas_call(
        functools.partial(pack_kernel, dims),
        out_shape=(
            jax.ShapeDtypeStruct((4, cells, snaps, nz), F32),
            jax.ShapeDtypeStruct((2, snaps * cells, nz), F32),
            x_face,
            x_face,
            y_face,
            y_face,
            z_face,
            z_face,
        ),
        in_specs=[HBM] * 4,
        out_specs=[VMEM] * 8,
        scratch_shapes=[
            pltpu.VMEM((4, snaps * cells, nz), BF16),
            pltpu.VMEM((2, snaps * cells, nz), F32),
            pltpu.SemaphoreType.DMA((4,)),
        ],
        compiler_params=params,
        name="pack",
    )(*flat)
    x0 = swapped(x0, "gx", 0)
    y0 = swapped(y0, "gy", 0)
    if sizes[1] > 2:
        y1 = swapped(y1, "gy", 1)
    z0 = swapped(z0, "gz", 0)
    z1 = swapped(z1, "gz", 1, True)
    if sizes[0] > 2:
        x1 = swapped(x1, "gx", 1)
    inner, select = pl.pallas_call(
        functools.partial(inner_kernel, dims),
        out_shape=(
            jax.ShapeDtypeStruct((4, cells, snaps, nz), F32),
            jax.ShapeDtypeStruct((nz, 2 * cells * nz), BF16),
        ),
        in_specs=[VMEM] * 2,
        out_specs=[VMEM] * 2,
        compiler_params=params,
        name="inner",
    )(fields, wide)
    scale = 1.0 / (2 * cells * nz * sizes[0] * sizes[1] * sizes[2])
    panel, moments = pl.pallas_call(
        functools.partial(panel_kernel, dims, scale, sizes),
        out_shape=(
            jax.ShapeDtypeStruct((2 * snaps, 2 * cells * nz), BF16),
            jax.ShapeDtypeStruct((snaps // 2, LANES), F32),
        ),
        in_specs=[VMEM] * 9,
        out_specs=[VMEM] * 2,
        compiler_params=params,
        name="panel",
    )(fields, inner, select, x0, x1, y0, y1, z0, z1)
    moments = summed(moments, mate)
    basis, factor = pl.pallas_call(
        functools.partial(basis_kernel, dims),
        out_shape=(
            jax.ShapeDtypeStruct((snaps * 2 * cells, nz), F32),
            jax.ShapeDtypeStruct((snaps, snaps), F32),
        ),
        in_specs=[VMEM] * 2,
        out_specs=[HBM, HBM],
        scratch_shapes=[
            pltpu.VMEM((snaps, LANES), F32),
            pltpu.VMEM((snaps, LANES), F32),
            pltpu.VMEM((snaps, snaps), F32),
            pltpu.VMEM((8 * snaps, LANES), F32),
            pltpu.VMEM((8 * snaps, LANES), F32),
            pltpu.VMEM((snaps * 2 * cells, nz), F32),
            pltpu.SemaphoreType.DMA((len(CUTS) + 1,)),
        ],
        compiler_params=params,
        name="basis",
    )(moments, panel)
    return basis.reshape(snaps, 2, nx, ny, nz), factor


def chip_mate(mesh):
    devices = list(mesh.devices.flat)
    at = [getattr(d, "coords", None) for d in devices]
    near = [k for k in range(1, len(at)) if at[0] is not None and at[k] == at[0]]
    return near[0] if near and near[0] & (near[0] - 1) == 0 else 1


def solution(mesh):
    spec = P(None, "gx", "gy", "gz")
    return jax.shard_map(
        functools.partial(per_device, chip_mate(mesh)),
        mesh=mesh,
        in_specs=(spec,) * 4,
        out_specs=(P(None, None, "gx", "gy", "gz"), P()),
        check_vma=False,
    )
```

```python
import functools

import jax
import jax.numpy as jnp
import numpy as np
from jax import lax
from jax.experimental import pallas as pl
from jax.experimental.pallas import tpu as pltpu
from jax.sharding import PartitionSpec as P

F32 = jnp.float32
BF16 = jnp.bfloat16
LANES = 128
CUTS = (0, 64)
VMEM = pl.BlockSpec(memory_space=pltpu.VMEM)
HBM = pl.BlockSpec(memory_space=pltpu.HBM)


AXES = ("gx", "gy", "gz")


def swapped(value, axis, first, periodic=False):
    sizes = [lax.axis_size(a) for a in AXES]
    where = AXES.index(axis)
    count = sizes[where]
    out = []
    for here in np.ndindex(*sizes):
        to = list(here)
        to[where] += 1 if here[where] % 2 == first else -1
        if periodic:
            to[where] %= count
        if not 0 <= to[where] < count:
            to = [here[0], here[1], here[2] ^ 1]
        out.append((int(np.ravel_multi_index(here, sizes)), int(np.ravel_multi_index(to, sizes))))
    return lax.ppermute(value, AXES, out)


def summed(value, mate):
    count = int(np.prod([lax.axis_size(a) for a in AXES]))
    if count & (count - 1):
        return lax.psum(value, AXES)

    def other(step):
        return lax.ppermute(value, AXES, [(i, i ^ step) for i in range(count)])

    steps = [1 << k for k in range(count.bit_length() - 1) if 1 << k != mate]
    steps = steps[-1:] + steps[:-1]
    value = value + other(mate)
    for k in range(0, len(steps) - 1, 2):
        near, far = steps[k : k + 2]
        one, two, both = other(near | mate), other(far | mate), other(near | far | mate)
        value = (value + one) + (two + both)
    if len(steps) % 2:
        value = value + other(steps[-1] | mate)
    return value


def lane_index(rows):
    return lax.broadcasted_iota(jnp.int32, (rows, LANES), 1)


def fold(full):
    full = jnp.concatenate([full, jnp.zeros((96, LANES - 96), F32)], axis=1)
    top, rest = full[0:48], full[48:96]
    lane = lane_index(48)
    near = pltpu.roll(rest, 48, 1)
    far = pltpu.roll(rest, 64, 1)
    top = jnp.where(lane >= 96, near, top)
    lane = lane_index(16)
    middle = jnp.where(lane < 16, near[32:48], top[16:32])
    bottom = jnp.where(lane < 16, near[0:16], jnp.where(lane < 32, far[16:32], top[32:48]))
    return jnp.concatenate([top[0:16], middle, bottom], axis=0)


def unfold(folded, work):
    lane = lane_index(16)
    near = pltpu.roll(folded, 80, 1)
    far = pltpu.roll(folded[32:48], 64, 1)
    work[0:48, :] = folded
    work[48:64, :] = jnp.where(lane < 80, near[0:16], near[32:48])
    work[64:80, :] = jnp.where(lane < 80, near[16:32], far)
    work[80:96, :] = jnp.where(lane < 80, near[32:48], near[16:32])


def row_of(wide, dims, f, r):
    return wide[f, pl.ds(r, dims[0], stride=dims[1] * dims[2]), :]


def sent_row(dims, f, r):
    x, y = divmod(r, dims[2])
    return f >= 2 or (x if f == 0 else y) in (0, dims[1 + f] - 1)


def pack_kernel(
    dims, u, v, w, rho, fields, wide, x0, x1, y0, y1, z0, z1, narrow, extra, arrived
):
    snaps, nx, ny = dims
    cells = nx * ny
    copies = [
        pltpu.make_async_copy(ref, narrow.at[f], arrived.at[f])
        for f, ref in enumerate((u, v, w, rho))
    ]
    for copy in copies:
        copy.start()
    x_even = lax.axis_index("gx") % 2 == 0
    y_even = lax.axis_index("gy") % 2 == 0
    z_even = lax.axis_index("gz") % 2 == 0
    lane = lane_index(snaps)
    column = jnp.zeros((snaps, LANES), F32)
    for f in range(4):
        copies[f].wait()
        from_rows = functools.partial(row_of, wide if f < 2 else extra, dims, f % 2)
        if f < 2:
            wide[f] = narrow[f].astype(F32)
        else:
            extra[f - 2] = narrow[f].astype(F32)
        for r in range(cells):
            if not sent_row(dims, f, r):
                continue
            value = from_rows(r)
            fields[f, r] = value
            if f >= 2:
                k = (f - 2) * cells + r
                moved = pltpu.roll(value, 2 * k + 1, 1)
                column = jnp.where((lane == 2 * k) | (lane == 2 * k + 1), moved, column)
        if f in (0, 3):
            for y in range(ny):
                first, final = fields[f, y], fields[f, (nx - 1) * ny + y]
                x0[f // 3, y] = jnp.where(x_even, final, first).astype(BF16)
                x1[f // 3, y] = jnp.where(x_even, first, final).astype(BF16)
        if f in (1, 3):
            for x in range(nx):
                first, final = fields[f, x * ny], fields[f, x * ny + ny - 1]
                y0[f // 3, x] = jnp.where(y_even, final, first).astype(BF16)
                y1[f // 3, x] = jnp.where(y_even, first, final).astype(BF16)
    final = jnp.where(lane % 2 == 0, column, 0.0)
    first = jnp.where(lane % 2 == 1, column, 0.0)
    z0[...] = jnp.where(z_even, final, first).astype(BF16)
    z1[...] = jnp.where(z_even, first, final).astype(BF16)


def inner_kernel(dims, fields, wide, inner, select):
    snaps, nx, ny = dims
    cells = nx * ny
    lane = lane_index(snaps)

    def row(f, r):
        return fields[f, r] if sent_row(dims, f, r) else row_of(wide, dims, f, r)

    sub = lax.broadcasted_iota(jnp.int32, (LANES, LANES), 0)
    at = lane_index(LANES)
    first, final = at == 0, at == LANES - 1
    for k in range(2 * cells):
        low = jnp.where(first & (sub == 2 * k), -1.0, 0.0)
        both = jnp.where(final & (sub == 2 * k + 1), 1.0, low)
        select[:, k * LANES : (k + 1) * LANES] = both.astype(BF16)

    def along(f, position, count, low, high):
        if position == 0:
            return row(f, high)
        if position == count - 1:
            return -row(f, low)
        return row(f, high) - row(f, low)

    def across(f, r):
        value = row(f, r)
        right = jnp.where(lane == LANES - 1, 0.0, pltpu.roll(value, LANES - 1, 1))
        return right - jnp.where(lane == 0, 0.0, pltpu.roll(value, 1, 1))

    for x in range(nx):
        for y in range(ny):
            r = x * ny + y
            inner[0, r] = (
                along(0, x, nx, r - ny, r + ny) + along(1, y, ny, r - 1, r + 1) + across(2, r)
            )
            inner[1, r] = along(3, x, nx, r - ny, r + ny)
            inner[2, r] = along(3, y, ny, r - 1, r + 1)
            inner[3, r] = across(3, r)


def panel_kernel(
    dims, scale, sizes, fields, inner, select, x0, x1, y0, y1, z0, z1, panel, moments
):
    snaps, nx, ny = dims
    cells = nx * ny
    at_x, at_y = lax.axis_index("gx"), lax.axis_index("gy")
    x_even, y_even = at_x % 2 == 0, at_y % 2 == 0
    edges = (z0[...].astype(F32) + z1[...].astype(F32)).astype(BF16)

    def outside(f, r, edge, received):
        return jnp.where(edge, fields[f, r], received.astype(F32))

    def add_x(value, f, i, x, y):
        if x == 0:
            received = jnp.where(x_even, x1[i, y], x0[i, y])
            value = value - outside(f, x * ny + y, at_x == 0, received)
        if x == nx - 1:
            received = jnp.where(x_even, x0[i, y], x1[i, y])
            value = value + outside(f, x * ny + y, at_x == sizes[0] - 1, received)
        return value

    def add_y(value, f, i, x, y):
        if y == 0:
            received = jnp.where(y_even, y1[i, x], y0[i, x])
            value = value - outside(f, x * ny + y, at_y == 0, received)
        if y == ny - 1:
            received = jnp.where(y_even, y0[i, x], y1[i, x])
            value = value + outside(f, x * ny + y, at_y == sizes[1] - 1, received)
        return value

    def add_z(value, i, r):
        k = i * cells + r
        near = jnp.dot(
            edges, select[:, k * LANES : (k + 1) * LANES], preferred_element_type=F32
        )
        return value + near

    def put(c, value):
        high = value.astype(BF16)
        panel[0:snaps, c * LANES : (c + 1) * LANES] = high
        panel[snaps : 2 * snaps, c * LANES : (c + 1) * LANES] = (
            value - high.astype(F32)
        ).astype(BF16)

    for x in range(nx):
        for y in range(ny):
            r = x * ny + y
            total = add_y(add_x(inner[0, r], 0, 0, x, y), 1, 0, x, y)
            put(r, 0.5 * add_z(total, 0, r))
            rx = add_x(inner[1, r], 3, 1, x, y)
            ry = add_y(inner[2, r], 3, 1, x, y)
            rz = add_z(inner[3, r], 1, r)
            put(cells + r, jnp.sqrt(0.25 * (rx * rx + ry * ry + rz * rz) + 0.25))

    def product(a, b):
        return lax.dot_general(a, b, (((1,), (1,)), ((), ())), preferred_element_type=F32)

    both = product(panel[...], panel[0:snaps, :])
    cross = both[snaps : 2 * snaps]
    total = (both[0:snaps] + cross + cross.T) * scale
    moments[...] = fold(total)


def basis_kernel(
    dims, moments, panel, basis, factor, work, inverse, upper, columns, held, ready, sent
):
    snaps, nx, ny = dims
    cells = 2 * nx * ny
    copies = []

    def emit(first, final):
        count = final - first
        exact = inverse[first:final, 0:snaps]
        high = exact.astype(BF16)
        rest = (exact - high.astype(F32)).astype(BF16)
        left = jnp.concatenate(
            [
                jnp.concatenate([high, high], axis=1),
                jnp.concatenate([rest, jnp.zeros_like(rest)], axis=1),
            ],
            axis=0,
        )
        for c in range(0, cells, 2):
            both = jnp.dot(left, panel[:, c * LANES : (c + 2) * LANES], preferred_element_type=F32)
            out = both[0:count] + both[count : 2 * count]
            for i in range(2):
                ready[pl.ds(first * cells + c + i, count, stride=cells), :] = out[
                    :, i * LANES : (i + 1) * LANES
                ]
        part = pl.ds(first * cells, count * cells)
        copies.append(
            pltpu.make_async_copy(ready.at[part], basis.at[part], sent.at[len(copies)])
        )
        copies[-1].start()

    lane = lane_index(8)
    sub = lax.broadcasted_iota(jnp.int32, (8, LANES), 0)
    groups = snaps // 8
    unfold(moments[...], work)

    def spread(value, j):
        return jnp.take_along_axis(value, jnp.full((8, LANES), j, jnp.int32), axis=1)

    def column_set(base):
        block = work[base : base + 8, :]
        return block, [spread(block, base + i) for i in range(8)]

    def repeat(base, block, cols):
        work[base : base + 8, :] = block
        for i in range(8):
            columns[8 * (base + i) : 8 * (base + i) + 8, :] = cols[i]
        corner = [
            [columns[pl.ds(8 * (base + i) + j, 8, stride=0), :] for j in range(i + 1)]
            for i in range(8)
        ]
        return [work[pl.ds(base + i, 8, stride=0), :] for i in range(8)], corner

    rows, small = repeat(0, *column_set(0))
    for g in range(groups):
        base = 8 * g
        inside = (lane >= base) & (lane < base + 8)
        last = g + 1 == groups
        if not last:
            block, cols = column_set(base + 8)
            block = jnp.where(inside, 0.0, block)
        outer = []
        done = jnp.zeros((8, LANES), F32)
        roots = jnp.zeros((8, LANES), F32)
        for j in range(8):
            here = base + j
            root = lax.rsqrt(small[j][j])
            inv = root * root
            pivot = jnp.where(lane == here, 1.0, rows[j])
            for i in range(j + 1, 8):
                m = small[i][j] * inv
                rows[i] = jnp.where(lane == here, 0.0, rows[i]) - m * pivot
                for k in range(j + 1, i + 1):
                    small[i][k] = small[i][k] - m * small[k][j]
            done = jnp.where(sub == j, rows[j] * root, done)
            roots = jnp.where(sub == j, root, roots)
            if last:
                continue
            clean = jnp.where((lane > here) & (lane < base + 8), 0.0, pivot) * inv
            outer.append(clean)
            m = jnp.take_along_axis(rows[j], sub + base + 8, axis=1)
            held[8 * here : 8 * here + 8, :] = m
            block = block - m * clean
            m = m * inv
            for i in range(8):
                cols[i] = cols[i] - m * held[pl.ds(8 * here + i, 8, stride=0), :]
        upper[base : base + 8, :] = jnp.where(lane >= sub + base, done, 0.0)[:, 0:snaps]
        inverse[base : base + 8, :] = jnp.where(
            lane < sub + base, done, jnp.where(lane == sub + base, roots, 0.0)
        )
        if last:
            break
        if base + 8 in CUTS:
            emit(CUTS[CUTS.index(base + 8) - 1], base + 8)
        rows_next, small = repeat(base + 8, block, cols)
        for h in range(g + 2, groups):
            block = jnp.where(inside, 0.0, work[8 * h : 8 * h + 8, :])
            for j in range(8):
                m = jnp.take_along_axis(rows[j], sub + 8 * h, axis=1)
                block = block - m * outer[j]
            work[8 * h : 8 * h + 8, :] = block
        rows = rows_next
    copies.append(pltpu.make_async_copy(upper, factor, sent.at[len(copies)]))
    copies[-1].start()
    emit(CUTS[-1], snaps)
    for copy in copies:
        copy.wait()


def per_device(mate, vel_u, vel_v, vel_w, density):
    snaps, nx, ny, nz = vel_u.shape
    cells = nx * ny
    dims = (snaps, nx, ny)
    sizes = tuple(lax.axis_size(a) for a in AXES)
    flat = [
        pltpu.with_memory_space_constraint(a.reshape(snaps * cells, nz), pltpu.HBM)
        for a in (vel_u, vel_v, vel_w, density)
    ]
    params = pltpu.CompilerParams(vmem_limit_bytes=12 << 20)
    x_face = jax.ShapeDtypeStruct((2, ny, snaps, nz), BF16)
    y_face = jax.ShapeDtypeStruct((2, nx, snaps, nz), BF16)
    z_face = jax.ShapeDtypeStruct((snaps, nz), BF16)
    fields, wide, x0, x1, y0, y1, z0, z1 = pl.pallas_call(
        functools.partial(pack_kernel, dims),
        out_shape=(
            jax.ShapeDtypeStruct((4, cells, snaps, nz), F32),
            jax.ShapeDtypeStruct((2, snaps * cells, nz), F32),
            x_face,
            x_face,
            y_face,
            y_face,
            z_face,
            z_face,
        ),
        in_specs=[HBM] * 4,
        out_specs=[VMEM] * 8,
        scratch_shapes=[
            pltpu.VMEM((4, snaps * cells, nz), BF16),
            pltpu.VMEM((2, snaps * cells, nz), F32),
            pltpu.SemaphoreType.DMA((4,)),
        ],
        compiler_params=params,
        name="pack",
    )(*flat)
    x0 = swapped(x0, "gx", 0)
    y0 = swapped(y0, "gy", 0)
    if sizes[1] > 2:
        y1 = swapped(y1, "gy", 1)
    z0 = swapped(z0, "gz", 0)
    z1 = swapped(z1, "gz", 1, True)
    if sizes[0] > 2:
        x1 = swapped(x1, "gx", 1)
    inner, select = pl.pallas_call(
        functools.partial(inner_kernel, dims),
        out_shape=(
            jax.ShapeDtypeStruct((4, cells, snaps, nz), F32),
            jax.ShapeDtypeStruct((nz, 2 * cells * nz), BF16),
        ),
        in_specs=[VMEM] * 2,
        out_specs=[VMEM] * 2,
        compiler_params=params,
        name="inner",
    )(fields, wide)
    scale = 1.0 / (2 * cells * nz * sizes[0] * sizes[1] * sizes[2])
    panel, moments = pl.pallas_call(
        functools.partial(panel_kernel, dims, scale, sizes),
        out_shape=(
            jax.ShapeDtypeStruct((2 * snaps, 2 * cells * nz), BF16),
            jax.ShapeDtypeStruct((snaps // 2, LANES), F32),
        ),
        in_specs=[VMEM] * 9,
        out_specs=[VMEM] * 2,
        compiler_params=params,
        name="panel",
    )(fields, inner, select, x0, x1, y0, y1, z0, z1)
    moments = summed(moments, mate)
    basis, factor = pl.pallas_call(
        functools.partial(basis_kernel, dims),
        out_shape=(
            jax.ShapeDtypeStruct((snaps * 2 * cells, nz), F32),
            jax.ShapeDtypeStruct((snaps, snaps), F32),
        ),
        in_specs=[VMEM] * 2,
        out_specs=[HBM, HBM],
        scratch_shapes=[
            pltpu.VMEM((snaps, LANES), F32),
            pltpu.VMEM((snaps, LANES), F32),
            pltpu.VMEM((snaps, snaps), F32),
            pltpu.VMEM((8 * snaps, LANES), F32),
            pltpu.VMEM((8 * snaps, LANES), F32),
            pltpu.VMEM((snaps * 2 * cells, nz), F32),
            pltpu.SemaphoreType.DMA((len(CUTS) + 1,)),
        ],
        compiler_params=params,
        name="basis",
    )(moments, panel)
    return basis.reshape(snaps, 2, nx, ny, nz), factor


def chip_mate(mesh):
    devices = list(mesh.devices.flat)
    at = [getattr(d, "coords", None) for d in devices]
    near = [k for k in range(1, len(at)) if at[0] is not None and at[k] == at[0]]
    return near[0] if near and near[0] & (near[0] - 1) == 0 else 1


def solution(mesh):
    spec = P(None, "gx", "gy", "gz")
    return jax.shard_map(
        functools.partial(per_device, chip_mate(mesh)),
        mesh=mesh,
        in_specs=(spec,) * 4,
        out_specs=(P(None, None, "gx", "gy", "gz"), P()),
        check_vma=False,
    )
```

```python
import functools

import jax
import jax.numpy as jnp
import numpy as np
from jax import lax
from jax.experimental import pallas as pl
from jax.experimental.pallas import tpu as pltpu
from jax.sharding import PartitionSpec as P

F32 = jnp.float32
BF16 = jnp.bfloat16
LANES = 128
CUTS = (0, 64)
VMEM = pl.BlockSpec(memory_space=pltpu.VMEM)
HBM = pl.BlockSpec(memory_space=pltpu.HBM)


AXES = ("gx", "gy", "gz")


def swapped(value, axis, first, periodic=False):
    sizes = [lax.axis_size(a) for a in AXES]
    where = AXES.index(axis)
    count = sizes[where]
    out = []
    for here in np.ndindex(*sizes):
        to = list(here)
        to[where] += 1 if here[where] % 2 == first else -1
        if periodic:
            to[where] %= count
        if not 0 <= to[where] < count:
            to = [here[0], here[1], here[2] ^ 1]
        out.append((int(np.ravel_multi_index(here, sizes)), int(np.ravel_multi_index(to, sizes))))
    return lax.ppermute(value, AXES, out)


def summed(value, mate):
    count = int(np.prod([lax.axis_size(a) for a in AXES]))
    if count & (count - 1):
        return lax.psum(value, AXES)

    def other(step):
        return lax.ppermute(value, AXES, [(i, i ^ step) for i in range(count)])

    steps = [1 << k for k in range(count.bit_length() - 1) if 1 << k != mate]
    steps = steps[-1:] + steps[:-1]
    value = value + other(mate)
    for k in range(0, len(steps) - 1, 2):
        near, far = steps[k : k + 2]
        one, two, both = other(near | mate), other(far | mate), other(near | far | mate)
        value = (value + one) + (two + both)
    if len(steps) % 2:
        value = value + other(steps[-1] | mate)
    return value


def lane_index(rows):
    return lax.broadcasted_iota(jnp.int32, (rows, LANES), 1)


def fold(full):
    full = jnp.concatenate([full, jnp.zeros((96, LANES - 96), F32)], axis=1)
    top, rest = full[0:48], full[48:96]
    lane = lane_index(48)
    near = pltpu.roll(rest, 48, 1)
    far = pltpu.roll(rest, 64, 1)
    top = jnp.where(lane >= 96, near, top)
    lane = lane_index(16)
    middle = jnp.where(lane < 16, near[32:48], top[16:32])
    bottom = jnp.where(lane < 16, near[0:16], jnp.where(lane < 32, far[16:32], top[32:48]))
    return jnp.concatenate([top[0:16], middle, bottom], axis=0)


def unfold(folded, work):
    lane = lane_index(16)
    near = pltpu.roll(folded, 80, 1)
    far = pltpu.roll(folded[32:48], 64, 1)
    work[0:48, :] = folded
    work[48:64, :] = jnp.where(lane < 80, near[0:16], near[32:48])
    work[64:80, :] = jnp.where(lane < 80, near[16:32], far)
    work[80:96, :] = jnp.where(lane < 80, near[32:48], near[16:32])


def row_of(wide, dims, f, r):
    return wide[f, pl.ds(r, dims[0], stride=dims[1] * dims[2]), :]


def sent_row(dims, f, r):
    x, y = divmod(r, dims[2])
    return f >= 2 or (x if f == 0 else y) in (0, dims[1 + f] - 1)


def pack_kernel(
    dims, two_ways, u, v, w, rho, fields, wide, x0, x1, y0, y1, z0, z1, narrow, extra, arrived
):
    snaps, nx, ny = dims
    cells = nx * ny
    copies = [
        pltpu.make_async_copy(ref, narrow.at[f], arrived.at[f])
        for f, ref in enumerate((u, v, w, rho))
    ]
    for copy in reversed(copies):
        copy.start()
    x_even = lax.axis_index("gx") % 2 == 0
    y_even = lax.axis_index("gy") % 2 == 0
    z_even = lax.axis_index("gz") % 2 == 0
    lane = lane_index(snaps)
    pair = lane // 2
    column = jnp.zeros((snaps, LANES), F32)
    for f in reversed(range(4)):
        copies[f].wait()
        from_rows = functools.partial(row_of, wide if f < 2 else extra, dims, f % 2)
        if f < 2:
            wide[f] = narrow[f].astype(F32)
        else:
            extra[f - 2] = narrow[f].astype(F32)
        for r in range(cells):
            if not sent_row(dims, f, r):
                continue
            value = from_rows(r)
            fields[f, r] = value
            if f >= 2:
                k = (f - 2) * cells + r
                moved = pltpu.roll(value, 2 * k + 1, 1)
                column = jnp.where(pair == k, moved, column)
        if f in (0, 3):
            for y in range(ny):
                first, final = fields[f, y], fields[f, (nx - 1) * ny + y]
                x0[f // 3, y] = jnp.where(x_even, final, first).astype(BF16)
                if two_ways:
                    x1[f // 3, y] = jnp.where(x_even, first, final).astype(BF16)
        if f in (1, 3):
            for x in range(nx):
                first, final = fields[f, x * ny], fields[f, x * ny + ny - 1]
                y0[f // 3, x] = jnp.where(y_even, final, first).astype(BF16)
                y1[f // 3, x] = jnp.where(y_even, first, final).astype(BF16)
    final = jnp.where(lane % 2 == 0, column, 0.0)
    first = jnp.where(lane % 2 == 1, column, 0.0)
    z0[...] = jnp.where(z_even, final, first).astype(BF16)
    z1[...] = jnp.where(z_even, first, final).astype(BF16)


def inner_kernel(dims, fields, wide, inner, select):
    snaps, nx, ny = dims
    cells = nx * ny
    lane = lane_index(snaps)

    def row(f, r):
        return fields[f, r] if sent_row(dims, f, r) else row_of(wide, dims, f, r)

    sub = lax.broadcasted_iota(jnp.int32, (LANES, LANES), 0)
    at = lane_index(LANES)
    first, final = at == 0, at == LANES - 1
    for k in range(2 * cells):
        low = jnp.where(first & (sub == 2 * k), -1.0, 0.0)
        both = jnp.where(final & (sub == 2 * k + 1), 1.0, low)
        select[:, k * LANES : (k + 1) * LANES] = both.astype(BF16)

    def along(f, position, count, low, high):
        if position == 0:
            return row(f, high)
        if position == count - 1:
            return -row(f, low)
        return row(f, high) - row(f, low)

    def across(f, r):
        value = row(f, r)
        right = jnp.where(lane == LANES - 1, 0.0, pltpu.roll(value, LANES - 1, 1))
        return right - jnp.where(lane == 0, 0.0, pltpu.roll(value, 1, 1))

    for x in range(nx):
        for y in range(ny):
            r = x * ny + y
            inner[0, r] = (
                along(0, x, nx, r - ny, r + ny) + along(1, y, ny, r - 1, r + 1) + across(2, r)
            )
            inner[1, r] = along(3, x, nx, r - ny, r + ny)
            inner[2, r] = along(3, y, ny, r - 1, r + 1)
            inner[3, r] = across(3, r)


def panel_kernel(
    dims, scale, sizes, fields, inner, select, x0, x1, y0, y1, z0, z1, panel, moments
):
    snaps, nx, ny = dims
    cells = nx * ny
    at_x, at_y = lax.axis_index("gx"), lax.axis_index("gy")
    x_even, y_even = at_x % 2 == 0, at_y % 2 == 0
    edges = (z0[...].astype(F32) + z1[...].astype(F32)).astype(BF16)

    def outside(f, r, edge, received):
        return jnp.where(edge, fields[f, r], received.astype(F32))

    def add_x(value, f, i, x, y):
        if x == 0:
            received = jnp.where(x_even, x1[i, y], x0[i, y]) if sizes[0] > 2 else x0[i, y]
            value = value - outside(f, x * ny + y, at_x == 0, received)
        if x == nx - 1:
            received = jnp.where(x_even, x0[i, y], x1[i, y]) if sizes[0] > 2 else x0[i, y]
            value = value + outside(f, x * ny + y, at_x == sizes[0] - 1, received)
        return value

    def add_y(value, f, i, x, y):
        if y == 0:
            received = jnp.where(y_even, y1[i, x], y0[i, x])
            value = value - outside(f, x * ny + y, at_y == 0, received)
        if y == ny - 1:
            received = jnp.where(y_even, y0[i, x], y1[i, x])
            value = value + outside(f, x * ny + y, at_y == sizes[1] - 1, received)
        return value

    near = {}

    def add_z(value, i, r):
        k = i * cells + r
        if k % 2 == 0:
            near[i] = jnp.dot(
                edges, select[:, k * LANES : (k + 2) * LANES], preferred_element_type=F32
            )
        return value + near[i][:, k % 2 * LANES : (k % 2 + 1) * LANES]

    def put(c, value):
        high = value.astype(BF16)
        panel[0:snaps, c * LANES : (c + 1) * LANES] = high
        panel[snaps : 2 * snaps, c * LANES : (c + 1) * LANES] = (
            value - high.astype(F32)
        ).astype(BF16)

    for x in range(nx):
        for y in range(ny):
            r = x * ny + y
            total = add_y(add_x(inner[0, r], 0, 0, x, y), 1, 0, x, y)
            put(r, 0.5 * add_z(total, 0, r))
            rx = add_x(inner[1, r], 3, 1, x, y)
            ry = add_y(inner[2, r], 3, 1, x, y)
            rz = add_z(inner[3, r], 1, r)
            put(cells + r, jnp.sqrt(0.25 * (rx * rx + ry * ry + rz * rz) + 0.25))

    def product(a, b):
        return lax.dot_general(a, b, (((1,), (1,)), ((), ())), preferred_element_type=F32)

    both = product(panel[...], panel[0:snaps, :])
    cross = both[snaps : 2 * snaps]
    total = (both[0:snaps] + cross + cross.T) * scale
    moments[...] = fold(total)


def basis_kernel(
    dims, moments, panel, basis, factor, work, inverse, upper, columns, held, ready, sent
):
    snaps, nx, ny = dims
    cells = 2 * nx * ny
    copies = []

    def emit(first, final):
        count = final - first
        exact = inverse[first:final, 0:snaps]
        high = exact.astype(BF16)
        rest = (exact - high.astype(F32)).astype(BF16)
        left = jnp.concatenate(
            [
                jnp.concatenate([high, high], axis=1),
                jnp.concatenate([rest, jnp.zeros_like(rest)], axis=1),
            ],
            axis=0,
        )
        for c in range(0, cells, 2):
            both = jnp.dot(left, panel[:, c * LANES : (c + 2) * LANES], preferred_element_type=F32)
            out = both[0:count] + both[count : 2 * count]
            for i in range(2):
                ready[pl.ds(first * cells + c + i, count, stride=cells), :] = out[
                    :, i * LANES : (i + 1) * LANES
                ]
        part = pl.ds(first * cells, count * cells)
        copies.append(
            pltpu.make_async_copy(ready.at[part], basis.at[part], sent.at[len(copies)])
        )
        copies[-1].start()

    lane = lane_index(8)
    sub = lax.broadcasted_iota(jnp.int32, (8, LANES), 0)
    groups = snaps // 8
    unfold(moments[...], work)

    def spread(value, j):
        return jnp.take_along_axis(value, jnp.full((8, LANES), j, jnp.int32), axis=1)

    def column_set(base):
        block = work[base : base + 8, :]
        return block, [spread(block, base + i) for i in range(8)]

    def repeat(base, block, cols):
        work[base : base + 8, :] = block
        for i in range(8):
            columns[8 * (base + i) : 8 * (base + i) + 8, :] = cols[i]
        corner = [
            [columns[pl.ds(8 * (base + i) + j, 8, stride=0), :] for j in range(i + 1)]
            for i in range(8)
        ]
        return [work[pl.ds(base + i, 8, stride=0), :] for i in range(8)], corner

    rows, small = repeat(0, *column_set(0))
    for g in range(groups):
        base = 8 * g
        inside = (lane >= base) & (lane < base + 8)
        last = g + 1 == groups
        if not last:
            block, cols = column_set(base + 8)
            block = jnp.where(inside, 0.0, block)
        outer = []
        done = jnp.zeros((8, LANES), F32)
        roots = jnp.zeros((8, LANES), F32)
        for j in range(8):
            here = base + j
            root = lax.rsqrt(small[j][j])
            inv = root * root
            pivot = jnp.where(lane == here, 1.0, rows[j])
            for i in range(j + 1, 8):
                m = small[i][j] * inv
                rows[i] = jnp.where(lane == here, 0.0, rows[i]) - m * pivot
                for k in range(j + 1, i + 1):
                    small[i][k] = small[i][k] - m * small[k][j]
            done = jnp.where(sub == j, rows[j] * root, done)
            roots = jnp.where(sub == j, root, roots)
            if last:
                continue
            clean = jnp.where((lane > here) & (lane < base + 8), 0.0, pivot) * inv
            outer.append(clean)
            m = jnp.take_along_axis(rows[j], sub + base + 8, axis=1)
            held[8 * here : 8 * here + 8, :] = m
            block = block - m * clean
            m = m * inv
            for i in range(8):
                cols[i] = cols[i] - m * held[pl.ds(8 * here + i, 8, stride=0), :]
        upper[base : base + 8, :] = jnp.where(lane >= sub + base, done, 0.0)[:, 0:snaps]
        inverse[base : base + 8, :] = jnp.where(
            lane < sub + base, done, jnp.where(lane == sub + base, roots, 0.0)
        )
        if last:
            break
        if base + 8 in CUTS:
            emit(CUTS[CUTS.index(base + 8) - 1], base + 8)
        rows_next, small = repeat(base + 8, block, cols)
        for h in range(g + 2, groups):
            block = jnp.where(inside, 0.0, work[8 * h : 8 * h + 8, :])
            for j in range(8):
                m = jnp.take_along_axis(rows[j], sub + 8 * h, axis=1)
                block = block - m * outer[j]
            work[8 * h : 8 * h + 8, :] = block
        rows = rows_next
    copies.append(pltpu.make_async_copy(upper, factor, sent.at[len(copies)]))
    copies[-1].start()
    emit(CUTS[-1], snaps)
    for copy in copies:
        copy.wait()


def per_device(mate, vel_u, vel_v, vel_w, density):
    snaps, nx, ny, nz = vel_u.shape
    cells = nx * ny
    dims = (snaps, nx, ny)
    sizes = tuple(lax.axis_size(a) for a in AXES)
    flat = [
        pltpu.with_memory_space_constraint(a.reshape(snaps * cells, nz), pltpu.HBM)
        for a in (vel_u, vel_v, vel_w, density)
    ]
    params = pltpu.CompilerParams(vmem_limit_bytes=12 << 20)
    x_face = jax.ShapeDtypeStruct((2, ny, snaps, nz), BF16)
    y_face = jax.ShapeDtypeStruct((2, nx, snaps, nz), BF16)
    z_face = jax.ShapeDtypeStruct((snaps, nz), BF16)
    fields, wide, x0, x1, y0, y1, z0, z1 = pl.pallas_call(
        functools.partial(pack_kernel, dims, sizes[0] > 2),
        out_shape=(
            jax.ShapeDtypeStruct((4, cells, snaps, nz), F32),
            jax.ShapeDtypeStruct((2, snaps * cells, nz), F32),
            x_face,
            x_face,
            y_face,
            y_face,
            z_face,
            z_face,
        ),
        in_specs=[HBM] * 4,
        out_specs=[VMEM] * 8,
        scratch_shapes=[
            pltpu.VMEM((4, snaps * cells, nz), BF16),
            pltpu.VMEM((2, snaps * cells, nz), F32),
            pltpu.SemaphoreType.DMA((4,)),
        ],
        compiler_params=params,
        name="pack",
    )(*flat)
    x0 = swapped(x0, "gx", 0)
    y0 = swapped(y0, "gy", 0)
    if sizes[1] > 2:
        y1 = swapped(y1, "gy", 1)
    z0 = swapped(z0, "gz", 0)
    z1 = swapped(z1, "gz", 1, True)
    if sizes[0] > 2:
        x1 = swapped(x1, "gx", 1)
    inner, select = pl.pallas_call(
        functools.partial(inner_kernel, dims),
        out_shape=(
            jax.ShapeDtypeStruct((4, cells, snaps, nz), F32),
            jax.ShapeDtypeStruct((nz, 2 * cells * nz), BF16),
        ),
        in_specs=[VMEM] * 2,
        out_specs=[VMEM] * 2,
        compiler_params=params,
        name="inner",
    )(fields, wide)
    scale = 1.0 / (2 * cells * nz * sizes[0] * sizes[1] * sizes[2])
    panel, moments = pl.pallas_call(
        functools.partial(panel_kernel, dims, scale, sizes),
        out_shape=(
            jax.ShapeDtypeStruct((2 * snaps, 2 * cells * nz), BF16),
            jax.ShapeDtypeStruct((snaps // 2, LANES), F32),
        ),
        in_specs=[VMEM] * 9,
        out_specs=[VMEM] * 2,
        compiler_params=params,
        name="panel",
    )(fields, inner, select, x0, x1, y0, y1, z0, z1)
    moments = summed(moments, mate)
    basis, factor = pl.pallas_call(
        functools.partial(basis_kernel, dims),
        out_shape=(
            jax.ShapeDtypeStruct((snaps * 2 * cells, nz), F32),
            jax.ShapeDtypeStruct((snaps, snaps), F32),
        ),
        in_specs=[VMEM] * 2,
        out_specs=[HBM, HBM],
        scratch_shapes=[
            pltpu.VMEM((snaps, LANES), F32),
            pltpu.VMEM((snaps, LANES), F32),
            pltpu.VMEM((snaps, snaps), F32),
            pltpu.VMEM((8 * snaps, LANES), F32),
            pltpu.VMEM((8 * snaps, LANES), F32),
            pltpu.VMEM((snaps * 2 * cells, nz), F32),
            pltpu.SemaphoreType.DMA((len(CUTS) + 1,)),
        ],
        compiler_params=params,
        name="basis",
    )(moments, panel)
    return basis.reshape(snaps, 2, nx, ny, nz), factor


def chip_mate(mesh):
    devices = list(mesh.devices.flat)
    at = [getattr(d, "coords", None) for d in devices]
    near = [k for k in range(1, len(at)) if at[0] is not None and at[k] == at[0]]
    return near[0] if near and near[0] & (near[0] - 1) == 0 else 1


def solution(mesh):
    spec = P(None, "gx", "gy", "gz")
    return jax.shard_map(
        functools.partial(per_device, chip_mate(mesh)),
        mesh=mesh,
        in_specs=(spec,) * 4,
        out_specs=(P(None, None, "gx", "gy", "gz"), P()),
        check_vma=False,
    )
```

```python
import functools

import jax
import jax.numpy as jnp
import numpy as np
from jax import lax
from jax.experimental import pallas as pl
from jax.experimental.pallas import tpu as pltpu
from jax.sharding import PartitionSpec as P

F32 = jnp.float32
BF16 = jnp.bfloat16
LANES = 128
CUTS = (0, 64)
VMEM = pl.BlockSpec(memory_space=pltpu.VMEM)
HBM = pl.BlockSpec(memory_space=pltpu.HBM)


AXES = ("gx", "gy", "gz")


def swapped(value, axis, first, periodic=False):
    sizes = [lax.axis_size(a) for a in AXES]
    where = AXES.index(axis)
    count = sizes[where]
    out = []
    for here in np.ndindex(*sizes):
        to = list(here)
        to[where] += 1 if here[where] % 2 == first else -1
        if periodic:
            to[where] %= count
        if not 0 <= to[where] < count:
            to = [here[0], here[1], here[2] ^ 1]
        out.append((int(np.ravel_multi_index(here, sizes)), int(np.ravel_multi_index(to, sizes))))
    return lax.ppermute(value, AXES, out)


def summed(value, mate):
    count = int(np.prod([lax.axis_size(a) for a in AXES]))
    if count & (count - 1):
        return lax.psum(value, AXES)

    def other(step):
        return lax.ppermute(value, AXES, [(i, i ^ step) for i in range(count)])

    steps = [1 << k for k in range(count.bit_length() - 1) if 1 << k != mate]
    steps = steps[-1:] + steps[:-1]
    value = value + other(mate)
    for k in range(0, len(steps) - 1, 2):
        near, far = steps[k : k + 2]
        one, two, both = other(near | mate), other(far | mate), other(near | far | mate)
        value = (value + one) + (two + both)
    if len(steps) % 2:
        value = value + other(steps[-1] | mate)
    return value


def lane_index(rows):
    return lax.broadcasted_iota(jnp.int32, (rows, LANES), 1)


def fold(full):
    full = jnp.concatenate([full, jnp.zeros((96, LANES - 96), F32)], axis=1)
    top, rest = full[0:48], full[48:96]
    lane = lane_index(48)
    near = pltpu.roll(rest, 48, 1)
    far = pltpu.roll(rest, 64, 1)
    top = jnp.where(lane >= 96, near, top)
    lane = lane_index(16)
    middle = jnp.where(lane < 16, near[32:48], top[16:32])
    bottom = jnp.where(lane < 16, near[0:16], jnp.where(lane < 32, far[16:32], top[32:48]))
    return jnp.concatenate([top[0:16], middle, bottom], axis=0)


def unfold(folded, work):
    lane = lane_index(16)
    near = pltpu.roll(folded, 80, 1)
    far = pltpu.roll(folded[32:48], 64, 1)
    work[0:48, :] = folded
    work[48:64, :] = jnp.where(lane < 80, near[0:16], near[32:48])
    work[64:80, :] = jnp.where(lane < 80, near[16:32], far)
    work[80:96, :] = jnp.where(lane < 80, near[32:48], near[16:32])


def row_of(wide, dims, f, r):
    return wide[f, pl.ds(r, dims[0], stride=dims[1] * dims[2]), :]


def sent_row(dims, f, r):
    x, y = divmod(r, dims[2])
    return f >= 2 or (x if f == 0 else y) in (0, dims[1 + f] - 1)


def pack_kernel(
    dims, two_ways, u, v, w, rho, fields, wide, x0, x1, y0, y1, z0, z1, narrow, extra, arrived
):
    snaps, nx, ny = dims
    cells = nx * ny
    copies = [
        pltpu.make_async_copy(ref, narrow.at[f], arrived.at[f])
        for f, ref in enumerate((u, v, w, rho))
    ]
    for copy in reversed(copies):
        copy.start()
    x_even = lax.axis_index("gx") % 2 == 0
    y_even = lax.axis_index("gy") % 2 == 0
    z_even = lax.axis_index("gz") % 2 == 0
    lane = lane_index(snaps)
    pair = lane // 2
    column = jnp.zeros((snaps, LANES), F32)
    for f in reversed(range(4)):
        copies[f].wait()
        from_rows = functools.partial(row_of, wide if f < 2 else extra, dims, f % 2)
        if f < 2:
            wide[f] = narrow[f].astype(F32)
        else:
            extra[f - 2] = narrow[f].astype(F32)
        for r in range(cells):
            if not sent_row(dims, f, r):
                continue
            value = from_rows(r)
            fields[f, r] = value
            if f >= 2:
                k = (f - 2) * cells + r
                moved = pltpu.roll(value, 2 * k + 1, 1)
                column = jnp.where(pair == k, moved, column)
        if f in (0, 3):
            for y in range(ny):
                first, final = fields[f, y], fields[f, (nx - 1) * ny + y]
                x0[f // 3, y] = jnp.where(x_even, final, first).astype(BF16)
                if two_ways:
                    x1[f // 3, y] = jnp.where(x_even, first, final).astype(BF16)
        if f in (1, 3):
            for x in range(nx):
                first, final = fields[f, x * ny], fields[f, x * ny + ny - 1]
                y0[f // 3, x] = jnp.where(y_even, final, first).astype(BF16)
                y1[f // 3, x] = jnp.where(y_even, first, final).astype(BF16)
    final = jnp.where(lane % 2 == 0, column, 0.0)
    first = jnp.where(lane % 2 == 1, column, 0.0)
    z0[...] = jnp.where(z_even, final, first).astype(BF16)
    z1[...] = jnp.where(z_even, first, final).astype(BF16)


def inner_kernel(dims, fields, wide, inner, select):
    snaps, nx, ny = dims
    cells = nx * ny
    lane = lane_index(snaps)

    def row(f, r):
        return fields[f, r] if sent_row(dims, f, r) else row_of(wide, dims, f, r)

    sub = lax.broadcasted_iota(jnp.int32, (LANES, LANES), 0)
    at = lane_index(LANES)
    first, final = at == 0, at == LANES - 1
    for k in range(2 * cells):
        low = jnp.where(first & (sub == 2 * k), -1.0, 0.0)
        both = jnp.where(final & (sub == 2 * k + 1), 1.0, low)
        select[:, k * LANES : (k + 1) * LANES] = both.astype(BF16)

    def along(f, position, count, low, high):
        if position == 0:
            return row(f, high)
        if position == count - 1:
            return -row(f, low)
        return row(f, high) - row(f, low)

    def across(f, r):
        value = row(f, r)
        right = jnp.where(lane == LANES - 1, 0.0, pltpu.roll(value, LANES - 1, 1))
        return right - jnp.where(lane == 0, 0.0, pltpu.roll(value, 1, 1))

    for x in range(nx):
        for y in range(ny):
            r = x * ny + y
            inner[0, r] = (
                along(0, x, nx, r - ny, r + ny) + along(1, y, ny, r - 1, r + 1) + across(2, r)
            )
            inner[1, r] = along(3, x, nx, r - ny, r + ny)
            inner[2, r] = along(3, y, ny, r - 1, r + 1)
            inner[3, r] = across(3, r)


def panel_kernel(
    dims, scale, sizes, fields, inner, select, x0, x1, y0, y1, z0, z1, panel, moments
):
    snaps, nx, ny = dims
    cells = nx * ny
    at_x, at_y = lax.axis_index("gx"), lax.axis_index("gy")
    x_even, y_even = at_x % 2 == 0, at_y % 2 == 0
    edges = (z0[...].astype(F32) + z1[...].astype(F32)).astype(BF16)

    def outside(f, r, edge, received):
        return jnp.where(edge, fields[f, r], received.astype(F32))

    def add_x(value, f, i, x, y):
        if x == 0:
            received = jnp.where(x_even, x1[i, y], x0[i, y]) if sizes[0] > 2 else x0[i, y]
            value = value - outside(f, x * ny + y, at_x == 0, received)
        if x == nx - 1:
            received = jnp.where(x_even, x0[i, y], x1[i, y]) if sizes[0] > 2 else x0[i, y]
            value = value + outside(f, x * ny + y, at_x == sizes[0] - 1, received)
        return value

    def add_y(value, f, i, x, y):
        if y == 0:
            received = jnp.where(y_even, y1[i, x], y0[i, x])
            value = value - outside(f, x * ny + y, at_y == 0, received)
        if y == ny - 1:
            received = jnp.where(y_even, y0[i, x], y1[i, x])
            value = value + outside(f, x * ny + y, at_y == sizes[1] - 1, received)
        return value

    near = {}

    def add_z(value, i, r):
        k = i * cells + r
        if k % 2 == 0:
            near[i] = jnp.dot(
                edges, select[:, k * LANES : (k + 2) * LANES], preferred_element_type=F32
            )
        return value + near[i][:, k % 2 * LANES : (k % 2 + 1) * LANES]

    def put(c, value):
        high = value.astype(BF16)
        panel[0:snaps, c * LANES : (c + 1) * LANES] = high
        panel[snaps : 2 * snaps, c * LANES : (c + 1) * LANES] = (
            value - high.astype(F32)
        ).astype(BF16)

    for x in range(nx):
        for y in range(ny):
            r = x * ny + y
            total = add_y(add_x(inner[0, r], 0, 0, x, y), 1, 0, x, y)
            put(r, 0.5 * add_z(total, 0, r))
            rx = add_x(inner[1, r], 3, 1, x, y)
            ry = add_y(inner[2, r], 3, 1, x, y)
            rz = add_z(inner[3, r], 1, r)
            square = 0.25 * (rx * rx + ry * ry + rz * rz) + 0.25
            put(cells + r, square * lax.rsqrt(square))

    def product(a, b):
        return lax.dot_general(a, b, (((1,), (1,)), ((), ())), preferred_element_type=F32)

    both = product(panel[...], panel[0:snaps, :])
    cross = both[snaps : 2 * snaps]
    total = (both[0:snaps] + cross + cross.T) * scale
    moments[...] = fold(total)


def basis_kernel(
    dims, moments, panel, basis, factor, work, inverse, upper, columns, held, ready, sent
):
    snaps, nx, ny = dims
    cells = 2 * nx * ny
    copies = []

    def emit(first, final):
        count = final - first
        exact = inverse[first:final, 0:snaps]
        high = exact.astype(BF16)
        rest = (exact - high.astype(F32)).astype(BF16)
        left = jnp.concatenate(
            [
                jnp.concatenate([high, high], axis=1),
                jnp.concatenate([rest, jnp.zeros_like(rest)], axis=1),
            ],
            axis=0,
        )
        for c in range(0, cells, 2):
            both = jnp.dot(left, panel[:, c * LANES : (c + 2) * LANES], preferred_element_type=F32)
            out = both[0:count] + both[count : 2 * count]
            for i in range(2):
                ready[pl.ds(first * cells + c + i, count, stride=cells), :] = out[
                    :, i * LANES : (i + 1) * LANES
                ]
        part = pl.ds(first * cells, count * cells)
        copies.append(
            pltpu.make_async_copy(ready.at[part], basis.at[part], sent.at[len(copies)])
        )
        copies[-1].start()

    lane = lane_index(8)
    sub = lax.broadcasted_iota(jnp.int32, (8, LANES), 0)
    groups = snaps // 8
    unfold(moments[...], work)

    def spread(value, j):
        return jnp.take_along_axis(value, jnp.full((8, LANES), j, jnp.int32), axis=1)

    def column_set(base):
        block = work[base : base + 8, :]
        return block, [spread(block, base + i) for i in range(8)]

    def repeat(base, block, cols):
        work[base : base + 8, :] = block
        for i in range(8):
            columns[8 * (base + i) : 8 * (base + i) + 8, :] = cols[i]
        corner = [
            [columns[pl.ds(8 * (base + i) + j, 8, stride=0), :] for j in range(i + 1)]
            for i in range(8)
        ]
        return [work[pl.ds(base + i, 8, stride=0), :] for i in range(8)], corner

    rows, small = repeat(0, *column_set(0))
    for g in range(groups):
        base = 8 * g
        inside = (lane >= base) & (lane < base + 8)
        last = g + 1 == groups
        if not last:
            block, cols = column_set(base + 8)
            block = jnp.where(inside, 0.0, block)
        outer = []
        done = jnp.zeros((8, LANES), F32)
        roots = jnp.zeros((8, LANES), F32)
        for j in range(8):
            here = base + j
            root = lax.rsqrt(small[j][j])
            inv = root * root
            pivot = jnp.where(lane == here, 1.0, rows[j])
            for i in range(j + 1, 8):
                m = small[i][j] * inv
                rows[i] = jnp.where(lane == here, 0.0, rows[i]) - m * pivot
                for k in range(j + 1, i + 1):
                    small[i][k] = small[i][k] - m * small[k][j]
            done = jnp.where(sub == j, rows[j] * root, done)
            roots = jnp.where(sub == j, root, roots)
            if last:
                continue
            clean = jnp.where((lane > here) & (lane < base + 8), 0.0, pivot) * inv
            outer.append(clean)
            m = jnp.take_along_axis(rows[j], sub + base + 8, axis=1)
            held[8 * here : 8 * here + 8, :] = m
            block = block - m * clean
            m = m * inv
            for i in range(8):
                cols[i] = cols[i] - m * held[pl.ds(8 * here + i, 8, stride=0), :]
        upper[base : base + 8, :] = jnp.where(lane >= sub + base, done, 0.0)[:, 0:snaps]
        inverse[base : base + 8, :] = jnp.where(
            lane < sub + base, done, jnp.where(lane == sub + base, roots, 0.0)
        )
        if last:
            break
        if base + 8 in CUTS:
            emit(CUTS[CUTS.index(base + 8) - 1], base + 8)
        rows_next, small = repeat(base + 8, block, cols)
        for h in range(g + 2, groups):
            block = jnp.where(inside, 0.0, work[8 * h : 8 * h + 8, :])
            for j in range(8):
                m = jnp.take_along_axis(rows[j], sub + 8 * h, axis=1)
                block = block - m * outer[j]
            work[8 * h : 8 * h + 8, :] = block
        rows = rows_next
    copies.append(pltpu.make_async_copy(upper, factor, sent.at[len(copies)]))
    copies[-1].start()
    emit(CUTS[-1], snaps)
    for copy in copies:
        copy.wait()


def per_device(mate, vel_u, vel_v, vel_w, density):
    snaps, nx, ny, nz = vel_u.shape
    cells = nx * ny
    dims = (snaps, nx, ny)
    sizes = tuple(lax.axis_size(a) for a in AXES)
    flat = [
        pltpu.with_memory_space_constraint(a.reshape(snaps * cells, nz), pltpu.HBM)
        for a in (vel_u, vel_v, vel_w, density)
    ]
    params = pltpu.CompilerParams(vmem_limit_bytes=12 << 20)
    x_face = jax.ShapeDtypeStruct((2, ny, snaps, nz), BF16)
    y_face = jax.ShapeDtypeStruct((2, nx, snaps, nz), BF16)
    z_face = jax.ShapeDtypeStruct((snaps, nz), BF16)
    fields, wide, x0, x1, y0, y1, z0, z1 = pl.pallas_call(
        functools.partial(pack_kernel, dims, sizes[0] > 2),
        out_shape=(
            jax.ShapeDtypeStruct((4, cells, snaps, nz), F32),
            jax.ShapeDtypeStruct((2, snaps * cells, nz), F32),
            x_face,
            x_face,
            y_face,
            y_face,
            z_face,
            z_face,
        ),
        in_specs=[HBM] * 4,
        out_specs=[VMEM] * 8,
        scratch_shapes=[
            pltpu.VMEM((4, snaps * cells, nz), BF16),
            pltpu.VMEM((2, snaps * cells, nz), F32),
            pltpu.SemaphoreType.DMA((4,)),
        ],
        compiler_params=params,
        name="pack",
    )(*flat)
    x0 = swapped(x0, "gx", 0)
    y0 = swapped(y0, "gy", 0)
    if sizes[1] > 2:
        y1 = swapped(y1, "gy", 1)
    z0 = swapped(z0, "gz", 0)
    z1 = swapped(z1, "gz", 1, True)
    if sizes[0] > 2:
        x1 = swapped(x1, "gx", 1)
    inner, select = pl.pallas_call(
        functools.partial(inner_kernel, dims),
        out_shape=(
            jax.ShapeDtypeStruct((4, cells, snaps, nz), F32),
            jax.ShapeDtypeStruct((nz, 2 * cells * nz), BF16),
        ),
        in_specs=[VMEM] * 2,
        out_specs=[VMEM] * 2,
        compiler_params=params,
        name="inner",
    )(fields, wide)
    scale = 1.0 / (2 * cells * nz * sizes[0] * sizes[1] * sizes[2])
    panel, moments = pl.pallas_call(
        functools.partial(panel_kernel, dims, scale, sizes),
        out_shape=(
            jax.ShapeDtypeStruct((2 * snaps, 2 * cells * nz), BF16),
            jax.ShapeDtypeStruct((snaps // 2, LANES), F32),
        ),
        in_specs=[VMEM] * 9,
        out_specs=[VMEM] * 2,
        compiler_params=params,
        name="panel",
    )(fields, inner, select, x0, x1, y0, y1, z0, z1)
    moments = summed(moments, mate)
    basis, factor = pl.pallas_call(
        functools.partial(basis_kernel, dims),
        out_shape=(
            jax.ShapeDtypeStruct((snaps * 2 * cells, nz), F32),
            jax.ShapeDtypeStruct((snaps, snaps), F32),
        ),
        in_specs=[VMEM] * 2,
        out_specs=[HBM, HBM],
        scratch_shapes=[
            pltpu.VMEM((snaps, LANES), F32),
            pltpu.VMEM((snaps, LANES), F32),
            pltpu.VMEM((snaps, snaps), F32),
            pltpu.VMEM((8 * snaps, LANES), F32),
            pltpu.VMEM((8 * snaps, LANES), F32),
            pltpu.VMEM((snaps * 2 * cells, nz), F32),
            pltpu.SemaphoreType.DMA((len(CUTS) + 1,)),
        ],
        compiler_params=params,
        name="basis",
    )(moments, panel)
    return basis.reshape(snaps, 2, nx, ny, nz), factor


def chip_mate(mesh):
    devices = list(mesh.devices.flat)
    at = [getattr(d, "coords", None) for d in devices]
    near = [k for k in range(1, len(at)) if at[0] is not None and at[k] == at[0]]
    return near[0] if near and near[0] & (near[0] - 1) == 0 else 1


def solution(mesh):
    spec = P(None, "gx", "gy", "gz")
    return jax.shard_map(
        functools.partial(per_device, chip_mate(mesh)),
        mesh=mesh,
        in_specs=(spec,) * 4,
        out_specs=(P(None, None, "gx", "gy", "gz"), P()),
        check_vma=False,
    )
```

```python
import functools

import jax
import jax.numpy as jnp
import numpy as np
from jax import lax
from jax.experimental import pallas as pl
from jax.experimental.pallas import tpu as pltpu
from jax.sharding import PartitionSpec as P

F32 = jnp.float32
BF16 = jnp.bfloat16
LANES = 128
CUTS = (0, 64)
VMEM = pl.BlockSpec(memory_space=pltpu.VMEM)
HBM = pl.BlockSpec(memory_space=pltpu.HBM)


AXES = ("gx", "gy", "gz")


def swapped(value, axis, first, periodic=False):
    sizes = [lax.axis_size(a) for a in AXES]
    where = AXES.index(axis)
    count = sizes[where]
    out = []
    for here in np.ndindex(*sizes):
        to = list(here)
        to[where] += 1 if here[where] % 2 == first else -1
        if periodic:
            to[where] %= count
        if not 0 <= to[where] < count:
            to = [here[0], here[1], here[2] ^ 1]
        out.append((int(np.ravel_multi_index(here, sizes)), int(np.ravel_multi_index(to, sizes))))
    return lax.ppermute(value, AXES, out)


def summed(value, mate):
    count = int(np.prod([lax.axis_size(a) for a in AXES]))
    if count & (count - 1):
        return lax.psum(value, AXES)

    def other(step):
        return lax.ppermute(value, AXES, [(i, i ^ step) for i in range(count)])

    steps = [1 << k for k in range(count.bit_length() - 1) if 1 << k != mate]
    steps = steps[-1:] + steps[:-1]
    value = value + other(mate)
    for k in range(0, len(steps) - 1, 2):
        near, far = steps[k : k + 2]
        one, two, both = other(near | mate), other(far | mate), other(near | far | mate)
        value = (value + one) + (two + both)
    if len(steps) % 2:
        value = value + other(steps[-1] | mate)
    return value


def lane_index(rows):
    return lax.broadcasted_iota(jnp.int32, (rows, LANES), 1)


def fold(full):
    full = jnp.concatenate([full, jnp.zeros((96, LANES - 96), F32)], axis=1)
    top, rest = full[0:48], full[48:96]
    lane = lane_index(48)
    near = pltpu.roll(rest, 48, 1)
    far = pltpu.roll(rest, 64, 1)
    top = jnp.where(lane >= 96, near, top)
    lane = lane_index(16)
    middle = jnp.where(lane < 16, near[32:48], top[16:32])
    bottom = jnp.where(lane < 16, near[0:16], jnp.where(lane < 32, far[16:32], top[32:48]))
    return jnp.concatenate([top[0:16], middle, bottom], axis=0)


def unfold(folded, work):
    lane = lane_index(16)
    near = pltpu.roll(folded, 80, 1)
    far = pltpu.roll(folded[32:48], 64, 1)
    work[0:48, :] = folded
    work[48:64, :] = jnp.where(lane < 80, near[0:16], near[32:48])
    work[64:80, :] = jnp.where(lane < 80, near[16:32], far)
    work[80:96, :] = jnp.where(lane < 80, near[32:48], near[16:32])


def row_of(wide, dims, f, r):
    return wide[f, pl.ds(r, dims[0], stride=dims[1] * dims[2]), :]


def sent_row(dims, f, r):
    x, y = divmod(r, dims[2])
    return f >= 2 or (x if f == 0 else y) in (0, dims[1 + f] - 1)


def pack_kernel(
    dims, two_ways, u, v, w, rho, fields, wide, x0, x1, y0, y1, z0, z1, narrow, extra, arrived
):
    snaps, nx, ny = dims
    cells = nx * ny
    copies = [
        pltpu.make_async_copy(ref, narrow.at[f], arrived.at[f])
        for f, ref in enumerate((u, v, w, rho))
    ]
    for copy in reversed(copies):
        copy.start()
    x_even = lax.axis_index("gx") % 2 == 0
    y_even = lax.axis_index("gy") % 2 == 0
    z_even = lax.axis_index("gz") % 2 == 0
    lane = lane_index(snaps)
    pair = lane // 2
    column = jnp.zeros((snaps, LANES), F32)
    for f in reversed(range(4)):
        copies[f].wait()
        from_rows = functools.partial(row_of, wide if f < 2 else extra, dims, f % 2)
        if f < 2:
            wide[f] = narrow[f].astype(F32)
        else:
            extra[f - 2] = narrow[f].astype(F32)
        for r in range(cells):
            if not sent_row(dims, f, r):
                continue
            value = from_rows(r)
            fields[f, r] = value
            if f >= 2:
                k = (f - 2) * cells + r
                moved = pltpu.roll(value, 2 * k + 1, 1)
                column = jnp.where(pair == k, moved, column)
        if f in (0, 3):
            for y in range(ny):
                first, final = fields[f, y], fields[f, (nx - 1) * ny + y]
                x0[f // 3, y] = jnp.where(x_even, final, first).astype(BF16)
                if two_ways:
                    x1[f // 3, y] = jnp.where(x_even, first, final).astype(BF16)
        if f in (1, 3):
            for x in range(nx):
                first, final = fields[f, x * ny], fields[f, x * ny + ny - 1]
                y0[f // 3, x] = jnp.where(y_even, final, first).astype(BF16)
                y1[f // 3, x] = jnp.where(y_even, first, final).astype(BF16)
    final = jnp.where(lane % 2 == 0, column, 0.0)
    first = jnp.where(lane % 2 == 1, column, 0.0)
    z0[...] = jnp.where(z_even, final, first).astype(BF16)
    z1[...] = jnp.where(z_even, first, final).astype(BF16)


def inner_kernel(dims, fields, wide, inner, select):
    snaps, nx, ny = dims
    cells = nx * ny
    lane = lane_index(snaps)

    def row(f, r):
        return fields[f, r] if sent_row(dims, f, r) else row_of(wide, dims, f, r)

    sub = lax.broadcasted_iota(jnp.int32, (LANES, LANES), 0)
    at = lane_index(LANES)
    first, final = at == 0, at == LANES - 1
    for k in range(2 * cells):
        low = jnp.where(first & (sub == 2 * k), -1.0, 0.0)
        both = jnp.where(final & (sub == 2 * k + 1), 1.0, low)
        select[:, k * LANES : (k + 1) * LANES] = both.astype(BF16)

    def along(f, position, count, low, high):
        if position == 0:
            return row(f, high)
        if position == count - 1:
            return -row(f, low)
        return row(f, high) - row(f, low)

    def across(f, r):
        value = row(f, r)
        right = jnp.where(lane == LANES - 1, 0.0, pltpu.roll(value, LANES - 1, 1))
        return right - jnp.where(lane == 0, 0.0, pltpu.roll(value, 1, 1))

    for x in range(nx):
        for y in range(ny):
            r = x * ny + y
            inner[0, r] = (
                along(0, x, nx, r - ny, r + ny) + along(1, y, ny, r - 1, r + 1) + across(2, r)
            )
            inner[1, r] = along(3, x, nx, r - ny, r + ny)
            inner[2, r] = along(3, y, ny, r - 1, r + 1)
            inner[3, r] = across(3, r)


def panel_kernel(
    dims, scale, sizes, fields, inner, select, x0, x1, y0, y1, z0, z1, panel, moments
):
    snaps, nx, ny = dims
    cells = nx * ny
    at_x, at_y = lax.axis_index("gx"), lax.axis_index("gy")
    x_even, y_even = at_x % 2 == 0, at_y % 2 == 0
    edges = (z0[...].astype(F32) + z1[...].astype(F32)).astype(BF16)

    def outside(f, r, edge, received):
        return jnp.where(edge, fields[f, r], received.astype(F32))

    def add_x(value, f, i, x, y):
        if x == 0:
            received = jnp.where(x_even, x1[i, y], x0[i, y]) if sizes[0] > 2 else x0[i, y]
            value = value - outside(f, x * ny + y, at_x == 0, received)
        if x == nx - 1:
            received = jnp.where(x_even, x0[i, y], x1[i, y]) if sizes[0] > 2 else x0[i, y]
            value = value + outside(f, x * ny + y, at_x == sizes[0] - 1, received)
        return value

    def add_y(value, f, i, x, y):
        if y == 0:
            received = jnp.where(y_even, y1[i, x], y0[i, x])
            value = value - outside(f, x * ny + y, at_y == 0, received)
        if y == ny - 1:
            received = jnp.where(y_even, y0[i, x], y1[i, x])
            value = value + outside(f, x * ny + y, at_y == sizes[1] - 1, received)
        return value

    near = {}

    def add_z(value, i, r):
        k = i * cells + r
        if k % 4 == 0:
            near[i] = jnp.dot(
                edges, select[:, k * LANES : (k + 4) * LANES], preferred_element_type=F32
            )
        return value + near[i][:, k % 4 * LANES : (k % 4 + 1) * LANES]

    def put(c, value):
        high = value.astype(BF16)
        panel[0:snaps, c * LANES : (c + 1) * LANES] = high
        panel[snaps : 2 * snaps, c * LANES : (c + 1) * LANES] = (
            value - high.astype(F32)
        ).astype(BF16)

    for x in range(nx):
        for y in range(ny):
            r = x * ny + y
            total = add_y(add_x(inner[0, r], 0, 0, x, y), 1, 0, x, y)
            put(r, 0.5 * add_z(total, 0, r))
            rx = add_x(inner[1, r], 3, 1, x, y)
            ry = add_y(inner[2, r], 3, 1, x, y)
            rz = add_z(inner[3, r], 1, r)
            square = 0.25 * (rx * rx + ry * ry + rz * rz) + 0.25
            put(cells + r, square * lax.rsqrt(square))

    def product(a, b):
        return lax.dot_general(a, b, (((1,), (1,)), ((), ())), preferred_element_type=F32)

    both = product(panel[...], panel[0:snaps, :])
    cross = both[snaps : 2 * snaps]
    total = (both[0:snaps] + cross + cross.T) * scale
    moments[...] = fold(total)


def basis_kernel(
    dims, moments, panel, basis, factor, work, inverse, upper, columns, held, ready, sent
):
    snaps, nx, ny = dims
    cells = 2 * nx * ny
    copies = []

    def emit(first, final):
        count = final - first
        exact = inverse[first:final, 0:snaps]
        high = exact.astype(BF16)
        rest = (exact - high.astype(F32)).astype(BF16)
        left = jnp.concatenate(
            [
                jnp.concatenate([high, high], axis=1),
                jnp.concatenate([rest, jnp.zeros_like(rest)], axis=1),
            ],
            axis=0,
        )
        for c in range(0, cells, 2):
            both = jnp.dot(left, panel[:, c * LANES : (c + 2) * LANES], preferred_element_type=F32)
            out = both[0:count] + both[count : 2 * count]
            for i in range(2):
                ready[pl.ds(first * cells + c + i, count, stride=cells), :] = out[
                    :, i * LANES : (i + 1) * LANES
                ]
        part = pl.ds(first * cells, count * cells)
        copies.append(
            pltpu.make_async_copy(ready.at[part], basis.at[part], sent.at[len(copies)])
        )
        copies[-1].start()

    lane = lane_index(8)
    sub = lax.broadcasted_iota(jnp.int32, (8, LANES), 0)
    groups = snaps // 8
    unfold(moments[...], work)

    def spread(value, j):
        return jnp.take_along_axis(value, jnp.full((8, LANES), j, jnp.int32), axis=1)

    def column_set(base):
        block = work[base : base + 8, :]
        return block, [spread(block, base + i) for i in range(8)]

    def repeat(base, block, cols):
        work[base : base + 8, :] = block
        for i in range(8):
            columns[8 * (base + i) : 8 * (base + i) + 8, :] = cols[i]
        corner = [
            [columns[pl.ds(8 * (base + i) + j, 8, stride=0), :] for j in range(i + 1)]
            for i in range(8)
        ]
        return [work[pl.ds(base + i, 8, stride=0), :] for i in range(8)], corner

    rows, small = repeat(0, *column_set(0))
    for g in range(groups):
        base = 8 * g
        inside = (lane >= base) & (lane < base + 8)
        last = g + 1 == groups
        if not last:
            block, cols = column_set(base + 8)
            block = jnp.where(inside, 0.0, block)
        outer = []
        done = jnp.zeros((8, LANES), F32)
        roots = jnp.zeros((8, LANES), F32)
        for j in range(8):
            here = base + j
            root = lax.rsqrt(small[j][j])
            inv = root * root
            pivot = jnp.where(lane == here, 1.0, rows[j])
            for i in range(j + 1, 8):
                m = small[i][j] * inv
                rows[i] = jnp.where(lane == here, 0.0, rows[i]) - m * pivot
                for k in range(j + 1, i + 1):
                    small[i][k] = small[i][k] - m * small[k][j]
            done = jnp.where(sub == j, rows[j] * root, done)
            roots = jnp.where(sub == j, root, roots)
            if last:
                continue
            clean = jnp.where((lane > here) & (lane < base + 8), 0.0, pivot) * inv
            outer.append(clean)
            m = jnp.take_along_axis(rows[j], sub + base + 8, axis=1)
            held[8 * here : 8 * here + 8, :] = m
            block = block - m * clean
            m = m * inv
            for i in range(8):
                cols[i] = cols[i] - m * held[pl.ds(8 * here + i, 8, stride=0), :]
        upper[base : base + 8, :] = jnp.where(lane >= sub + base, done, 0.0)[:, 0:snaps]
        inverse[base : base + 8, :] = jnp.where(
            lane < sub + base, done, jnp.where(lane == sub + base, roots, 0.0)
        )
        if last:
            break
        if base + 8 in CUTS:
            emit(CUTS[CUTS.index(base + 8) - 1], base + 8)
        rows_next, small = repeat(base + 8, block, cols)
        for h in range(g + 2, groups):
            block = jnp.where(inside, 0.0, work[8 * h : 8 * h + 8, :])
            for j in range(8):
                m = jnp.take_along_axis(rows[j], sub + 8 * h, axis=1)
                block = block - m * outer[j]
            work[8 * h : 8 * h + 8, :] = block
        rows = rows_next
    copies.append(pltpu.make_async_copy(upper, factor, sent.at[len(copies)]))
    copies[-1].start()
    emit(CUTS[-1], snaps)
    for copy in copies:
        copy.wait()


def per_device(mate, vel_u, vel_v, vel_w, density):
    snaps, nx, ny, nz = vel_u.shape
    cells = nx * ny
    dims = (snaps, nx, ny)
    sizes = tuple(lax.axis_size(a) for a in AXES)
    flat = [
        pltpu.with_memory_space_constraint(a.reshape(snaps * cells, nz), pltpu.HBM)
        for a in (vel_u, vel_v, vel_w, density)
    ]
    params = pltpu.CompilerParams(vmem_limit_bytes=12 << 20)
    x_face = jax.ShapeDtypeStruct((2, ny, snaps, nz), BF16)
    y_face = jax.ShapeDtypeStruct((2, nx, snaps, nz), BF16)
    z_face = jax.ShapeDtypeStruct((snaps, nz), BF16)
    fields, wide, x0, x1, y0, y1, z0, z1 = pl.pallas_call(
        functools.partial(pack_kernel, dims, sizes[0] > 2),
        out_shape=(
            jax.ShapeDtypeStruct((4, cells, snaps, nz), F32),
            jax.ShapeDtypeStruct((2, snaps * cells, nz), F32),
            x_face,
            x_face,
            y_face,
            y_face,
            z_face,
            z_face,
        ),
        in_specs=[HBM] * 4,
        out_specs=[VMEM] * 8,
        scratch_shapes=[
            pltpu.VMEM((4, snaps * cells, nz), BF16),
            pltpu.VMEM((2, snaps * cells, nz), F32),
            pltpu.SemaphoreType.DMA((4,)),
        ],
        compiler_params=params,
        name="pack",
    )(*flat)
    x0 = swapped(x0, "gx", 0)
    y0 = swapped(y0, "gy", 0)
    if sizes[1] > 2:
        y1 = swapped(y1, "gy", 1)
    z0 = swapped(z0, "gz", 0)
    z1 = swapped(z1, "gz", 1, True)
    if sizes[0] > 2:
        x1 = swapped(x1, "gx", 1)
    inner, select = pl.pallas_call(
        functools.partial(inner_kernel, dims),
        out_shape=(
            jax.ShapeDtypeStruct((4, cells, snaps, nz), F32),
            jax.ShapeDtypeStruct((nz, 2 * cells * nz), BF16),
        ),
        in_specs=[VMEM] * 2,
        out_specs=[VMEM] * 2,
        compiler_params=params,
        name="inner",
    )(fields, wide)
    scale = 1.0 / (2 * cells * nz * sizes[0] * sizes[1] * sizes[2])
    panel, moments = pl.pallas_call(
        functools.partial(panel_kernel, dims, scale, sizes),
        out_shape=(
            jax.ShapeDtypeStruct((2 * snaps, 2 * cells * nz), BF16),
            jax.ShapeDtypeStruct((snaps // 2, LANES), F32),
        ),
        in_specs=[VMEM] * 9,
        out_specs=[VMEM] * 2,
        compiler_params=params,
        name="panel",
    )(fields, inner, select, x0, x1, y0, y1, z0, z1)
    moments = summed(moments, mate)
    basis, factor = pl.pallas_call(
        functools.partial(basis_kernel, dims),
        out_shape=(
            jax.ShapeDtypeStruct((snaps * 2 * cells, nz), F32),
            jax.ShapeDtypeStruct((snaps, snaps), F32),
        ),
        in_specs=[VMEM] * 2,
        out_specs=[HBM, HBM],
        scratch_shapes=[
            pltpu.VMEM((snaps, LANES), F32),
            pltpu.VMEM((snaps, LANES), F32),
            pltpu.VMEM((snaps, snaps), F32),
            pltpu.VMEM((8 * snaps, LANES), F32),
            pltpu.VMEM((8 * snaps, LANES), F32),
            pltpu.VMEM((snaps * 2 * cells, nz), F32),
            pltpu.SemaphoreType.DMA((len(CUTS) + 1,)),
        ],
        compiler_params=params,
        name="basis",
    )(moments, panel)
    return basis.reshape(snaps, 2, nx, ny, nz), factor


def chip_mate(mesh):
    devices = list(mesh.devices.flat)
    at = [getattr(d, "coords", None) for d in devices]
    near = [k for k in range(1, len(at)) if at[0] is not None and at[k] == at[0]]
    return near[0] if near and near[0] & (near[0] - 1) == 0 else 1


def solution(mesh):
    spec = P(None, "gx", "gy", "gz")
    return jax.shard_map(
        functools.partial(per_device, chip_mate(mesh)),
        mesh=mesh,
        in_specs=(spec,) * 4,
        out_specs=(P(None, None, "gx", "gy", "gz"), P()),
        check_vma=False,
    )
```
